512 devices in a mesh: member: 16 (over x, z_hi), slab: 32 (over y, z_lo, core).
Axes of the slice: x: 4, y: 4, z: 16 (z_hi: 4, z_lo: 4; z = z_hi * 4 + z_lo), core: 2. Of those that a mesh axis runs over, the one named last changes fastest.
Arguments:
- fluid_head_start: float32 [192, 512, 128], P('member', 'slab'), may hold values from -6 to 6
- conductivity_matrix: float32 [192, 512, 128], P('member', 'slab'), may hold values from 0.1 to 1
- well_rates: float32 [512, 128], P('slab'), may hold values from -3 to 3
- cell_layer: int32 [512, 128], P('slab'), may hold values from 0 to 7
- pixel_coords: int32 [2, 4096], replicated, may hold values from 0 to 63
- obs_index: int32 [1024], replicated, may hold values from 0 to 4095
- obs_value: float32 [1024], replicated, may hold values from -0.6 to 0.6
- obs_sigma: float32 [1024], replicated, may hold values from 0.05 to 0.5
Outputs:
- analysed: float32 [192, 512, 128], P('member', 'slab')
- subsidence: float32 [4096, 192], P(('member', 'slab'))
The draws below stay inside these ranges and needn't reach their ends.
All inputs are finite; a program needn't handle non-finite values.
Results may differ from the reference program's by a relative error of at most 0.00028.
Values sent between devices are 32-bit elements; how exact they have to be, the bound alone decides.
A program may use at most 64 MiB of HBM per device.

```python
import math
import jax
import jax.numpy as jnp
from jax import lax

E = 192
AQUIFER_BREADTH = 128
STEPS = 4
P_SIZE = 4096
M = 1024
AQUIFER_LINES = 512


def set_ends(values, rng, least, largest):
    shape = values.shape
    place = [jax.random.randint(jax.random.fold_in(rng, axis), (), 0, shape[axis]) for axis in range(len(shape))]
    values = values.at[tuple(place)].set(least)
    longest = shape.index(max(shape))
    place[longest] = (place[longest] + 1) % shape[longest]
    return values.at[tuple(place)].set(largest)


def block_scale(own_key, extent, split, smallest, top_value):
    def one(axis_at, blocks):
        heights = jax.random.uniform(jax.random.fold_in(jax.random.fold_in(own_key, 6), axis_at), (blocks,), jnp.float32, smallest / len(split), top_value / len(split))
        return jnp.repeat(jnp.exp(heights), extent[axis_at] // blocks).reshape((-1,) + (1,) * (len(extent) - axis_at - 1))

    loudness = one(*split[0])
    for cut in split[1:]:
        loudness = loudness * one(*cut)
    return loudness


def normal_values(stream_key, shape, deviation, reach, cuts=(), held_as=jnp.bfloat16):
    loudness = block_scale(stream_key, shape, cuts, -0.22, 0.18) if cuts else 1.0
    entries = jax.random.normal(stream_key, shape, jnp.float32) * deviation * loudness
    return jnp.minimum(jnp.maximum(entries, -reach), reach).astype(held_as)


def setup_inputs(seed: int = 0) -> dict:
    streams_of = jax.random.split(jax.random.key(seed), 9)
    return {
        "fluid_head_start": normal_values(streams_of[0], (E, AQUIFER_LINES, AQUIFER_BREADTH), 1.0, 6.0, ((0, 16), (1, 32)), jnp.float32),
        "conductivity_matrix": jnp.clip(jnp.exp(math.log(1.0) - 2.3025851 * jax.random.uniform(streams_of[1], (E, AQUIFER_LINES, AQUIFER_BREADTH), jnp.float32) ** block_scale(streams_of[1], (E, AQUIFER_LINES, AQUIFER_BREADTH), ((0, 16), (1, 32)), -0.2, 0.2)), 0.1, 1.0),
        "well_rates": normal_values(streams_of[2], (AQUIFER_LINES, AQUIFER_BREADTH), 0.5, 3.0, ((0, 32),), jnp.float32),
        "cell_layer": set_ends(jax.random.randint(streams_of[3], (AQUIFER_LINES, AQUIFER_BREADTH), 0, 8), jax.random.fold_in(streams_of[3], 1), 0, 7).astype(jnp.int32),
        "pixel_coords": set_ends(jax.random.randint(streams_of[4], (2, P_SIZE), 0, 64), jax.random.fold_in(streams_of[4], 1), 0, 63).astype(jnp.int32),
        "obs_index": set_ends(jax.random.randint(streams_of[5], (M,), 0, P_SIZE), jax.random.fold_in(streams_of[5], 1), 0, P_SIZE - 1).astype(jnp.int32),
        "obs_value": normal_values(streams_of[6], (M,), 0.1, 0.6, (), jnp.float32),
        "obs_sigma": jnp.clip(jnp.exp(jax.random.uniform(streams_of[7], (M,), jnp.float32, math.log(0.05), math.log(0.5))), 0.05, 0.5),
    }


time_step = 0.15
pixel_span = 64.0
top_depth = 2.0

def advance_in_time(fluid_head_grid, perm_field, source, open_faces):
    mobility = perm_field * (1.0 + 0.5 * jnp.tanh(fluid_head_grid))
    sample_vectors, height, across_cells = fluid_head_grid.shape
    across = 0.5 * (mobility[:, 1:] + mobility[:, :-1]) * open_faces[None, :, None]
    flux_rows = across * (fluid_head_grid[:, 1:] - fluid_head_grid[:, :-1])
    zero_row = jnp.zeros((sample_vectors, 1, across_cells), fluid_head_grid.dtype)
    inflow = jnp.concatenate([flux_rows, zero_row], 1) - jnp.concatenate([zero_row, flux_rows], 1)
    along = 0.5 * (mobility[:, :, 1:] + mobility[:, :, :-1])
    flux_cols = along * (fluid_head_grid[:, :, 1:] - fluid_head_grid[:, :, :-1])
    zero_col = jnp.zeros((sample_vectors, height, 1), fluid_head_grid.dtype)
    inflow = inflow + (jnp.concatenate([flux_cols, zero_col], 2) - jnp.concatenate([zero_col, flux_cols], 2))
    return fluid_head_grid + time_step * (inflow + source[None])

def kernel_rows(pixel_x, pixel_y, cell_x, cell_y, depth, volume):
    delta_x = cell_x[None, :] - pixel_x[:, None]
    delta_y = cell_y[None, :] - pixel_y[:, None]
    radius = delta_x * delta_x + delta_y * delta_y + depth[None, :] * depth[None, :]
    return volume * depth[None, :] / (radius * jnp.sqrt(radius))

def gram_terms(predicted, obs_value, obs_sigma, owned):
    centre = lax.optimization_barrier(jnp.mean(predicted, axis=1))
    anomaly = predicted - centre[:, None]
    inverse_var = 1.0 / (obs_sigma * obs_sigma)
    weighted = anomaly * inverse_var[:, None]
    gram = lax.dot_general(anomaly, weighted, (((0,), (0,)), ((), ())), precision=lax.Precision.HIGHEST)
    rhs = jnp.dot(owned * (obs_value - centre), weighted, precision=lax.Precision.HIGHEST)
    return (gram, rhs)

def finish(gram, rhs, sample_vector_pile):
    sample_vectors = sample_vector_pile.shape[0]
    ident = jnp.eye(sample_vectors, dtype=gram.dtype)
    gram = gram + (sample_vectors - 1.0) * ident
    factor = jnp.linalg.cholesky(gram)
    inverse = jax.scipy.linalg.solve_triangular(factor, ident, lower=True)
    weights = jnp.dot(inverse.T, jnp.dot(inverse, rhs, precision=lax.Precision.HIGHEST), precision=lax.Precision.HIGHEST)
    transform = jnp.sqrt(sample_vectors - 1.0) * inverse.T
    mix = weights[:, None] + transform
    centre = lax.optimization_barrier(jnp.mean(sample_vector_pile, axis=0))
    spread = sample_vector_pile - centre[None]
    return centre[None] + lax.dot_general(mix, spread, (((0,), (0,)), ((), ())), precision=lax.Precision.HIGHEST)

def reference(fluid_head_start, conductivity_matrix, well_rates, cell_layer, pixel_coords, obs_index, obs_value, obs_sigma):
    open_faces = jnp.ones((AQUIFER_LINES - 1,), jnp.float32)

    def evolve_sample(pair):
        fluid_head_grid = pair[0][None]
        perm_field = pair[1][None]
        for repeat in range(STEPS):
            fluid_head_grid = advance_in_time(fluid_head_grid, perm_field, well_rates, open_faces)
        return fluid_head_grid[0]
    predicted_ensemble = lax.map(evolve_sample, (fluid_head_start, conductivity_matrix))
    sample_vectors = predicted_ensemble.shape[0]
    volume = pixel_span * pixel_span / (AQUIFER_LINES * AQUIFER_BREADTH)
    row_pos = (jnp.arange(AQUIFER_LINES).astype(jnp.float32) + 0.5) * (pixel_span / AQUIFER_LINES)
    col_pos = (jnp.arange(AQUIFER_BREADTH).astype(jnp.float32) + 0.5) * (pixel_span / AQUIFER_BREADTH)
    pixel_f = pixel_coords.astype(jnp.float32)
    lines_in_slab_part = math.gcd(AQUIFER_LINES, 16)

    def add_block(index, total):
        topmost_line = (index * lines_in_slab_part).astype(jnp.int32)
        sample_vector_pile = lax.dynamic_slice_in_dim(predicted_ensemble, topmost_line, lines_in_slab_part, 1).reshape(sample_vectors, lines_in_slab_part * AQUIFER_BREADTH)
        layers = lax.dynamic_slice_in_dim(cell_layer, topmost_line, lines_in_slab_part, 0).astype(jnp.float32)
        depth = (top_depth + layers).reshape(-1)
        rows_here = lax.dynamic_slice_in_dim(row_pos, topmost_line, lines_in_slab_part, 0)
        cell_x = jnp.broadcast_to(rows_here[:, None], (lines_in_slab_part, AQUIFER_BREADTH)).reshape(-1)
        cell_y = jnp.broadcast_to(col_pos[None, :], (lines_in_slab_part, AQUIFER_BREADTH)).reshape(-1)
        kern = kernel_rows(pixel_f[0], pixel_f[1], cell_x, cell_y, depth, volume)
        return total + lax.dot_general(kern, sample_vector_pile, (((1,), (1,)), ((), ())), precision=lax.Precision.HIGHEST)
    subsidence = lax.fori_loop(0, AQUIFER_LINES // lines_in_slab_part, add_block, jnp.zeros((P_SIZE, sample_vectors), jnp.float32))
    predicted = jnp.take(subsidence, obs_index, axis=0)
    gram, rhs = gram_terms(predicted, obs_value, obs_sigma, jnp.ones_like(obs_value))
    sample_vector_pile = predicted_ensemble.reshape(sample_vectors, AQUIFER_LINES * AQUIFER_BREADTH)
    analysed = finish(gram, rhs, sample_vector_pile).reshape(sample_vectors, AQUIFER_LINES, AQUIFER_BREADTH)
    return (analysed, subsidence)
```

```python
import math

import jax
import jax.numpy as jnp
from jax import lax
from jax.experimental import pallas as pl
from jax.experimental.pallas import tpu as pltpu
from jax.sharding import PartitionSpec as P

STEPS = 4
time_step = 0.15
pixel_span = 64.0
top_depth = 2.0
F32 = jnp.float32
BF16 = jnp.bfloat16
HIGHEST = lax.Precision.HIGHEST
BLOCK = 256


def padded(value, sides, width):
    for axis, dim in sides:
        size, length = (lax.axis_size(axis), value.shape[dim])
        up = [(i, (i + 1) % size) for i in range(size - 1)]
        down = [(j, i) for i, j in up]
        last = lax.slice_in_dim(value, length - width, length, axis=dim)
        initial = lax.slice_in_dim(value, 0, width, axis=dim)
        before = lax.ppermute(last, axis, up)
        after = lax.ppermute(initial, axis, down)
        value = jnp.concatenate([before, value, after], axis=dim)
    return value


def advance_in_time(fluid_head_grid, perm_field, source, open_faces):
    mobility = perm_field * (1.0 + 0.5 * jnp.tanh(fluid_head_grid))
    sample_vectors, height, across_cells = fluid_head_grid.shape
    across = 0.5 * (mobility[:, 1:] + mobility[:, :-1]) * open_faces[None, :, None]
    flux_rows = across * (fluid_head_grid[:, 1:] - fluid_head_grid[:, :-1])
    zero_row = jnp.zeros((sample_vectors, 1, across_cells), fluid_head_grid.dtype)
    inflow = jnp.concatenate([flux_rows, zero_row], 1) - jnp.concatenate([zero_row, flux_rows], 1)
    along = 0.5 * (mobility[:, :, 1:] + mobility[:, :, :-1])
    flux_cols = along * (fluid_head_grid[:, :, 1:] - fluid_head_grid[:, :, :-1])
    zero_col = jnp.zeros((sample_vectors, height, 1), fluid_head_grid.dtype)
    inflow = inflow + (
        jnp.concatenate([flux_cols, zero_col], 2) - jnp.concatenate([zero_col, flux_cols], 2)
    )
    return fluid_head_grid + time_step * (inflow + source[None])


def face_mask(first_global, height, total_rows):
    index = first_global + jnp.arange(height - 1, dtype=jnp.int32)
    return ((index >= 0) & (index + 1 <= total_rows - 1)).astype(jnp.float32)


def split(value):
    high = value.astype(BF16)
    return high, (value - high.astype(F32)).astype(BF16)


def twice(value):
    return jnp.concatenate([value, value], axis=1)


def subsidence_kernel(volume, row_pitch, col_pitch, f_ref, lay_ref, pc_ref, out_ref, w_ref, h2_ref, vh_ref):
    slab = lax.axis_index("slab")
    members = f_ref.shape[0]
    rows, cols = lay_ref.shape
    high, low = split(f_ref[...])
    w_ref[...] = jnp.zeros_like(w_ref)
    w_ref[0:members, :] = high
    w_ref[16 : 16 + members, :] = low
    depth = top_depth + lay_ref[...].astype(F32)
    depth = jnp.concatenate([depth, jnp.zeros((cols - rows, cols), F32)], axis=0).T
    for i in range(rows):
        column = depth[:, i : i + 1]
        h2_ref[i] = jnp.broadcast_to(column * column, (cols, 128))
        vh_ref[i] = jnp.broadcast_to(volume * column, (cols, 128))
    cell_y = (lax.broadcasted_iota(jnp.int32, (cols, BLOCK), 0).astype(F32) + 0.5) * col_pitch
    first = (slab * rows).astype(F32)

    def block(b, carry):
        at = pl.multiple_of(b * BLOCK, BLOCK)
        coords = pc_ref[:, pl.ds(at, BLOCK)].astype(F32)
        delta_y = cell_y - coords[1:2]
        dy2 = delta_y * delta_y
        total = jnp.zeros((32, BLOCK), F32)
        for pair in range(rows // 2):
            tiles = []
            for i in (2 * pair, 2 * pair + 1):
                delta_x = (first + (i + 0.5)) * row_pitch - coords[0:1]
                radius = (dy2 + delta_x * delta_x) + twice(h2_ref[i])
                inv = lax.rsqrt(radius)
                tiles.append(twice(vh_ref[i]) * (inv * inv * inv))
            high, low = split(jnp.concatenate(tiles, axis=0))
            weights = w_ref[:, 256 * pair : 256 * pair + 256]
            total += jnp.dot(weights, high, preferred_element_type=F32)
            total += jnp.dot(weights, low, preferred_element_type=F32)
        out_ref[:, pl.ds(at, BLOCK)] = total[0:16] + total[16:32]
        return carry

    lax.fori_loop(0, pc_ref.shape[1] // BLOCK, block, 0)


def subsidence_partial(forecast, cell_layer, coords, total_rows):
    members, rows, cols = forecast.shape
    pixels = coords.shape[1]
    volume = pixel_span * pixel_span / (total_rows * cols)
    body = lambda *refs: subsidence_kernel(volume, pixel_span / total_rows, pixel_span / cols, *refs)
    return pl.pallas_call(
        body,
        name="subsidence",
        out_shape=jax.ShapeDtypeStruct((16, pixels), F32),
        in_specs=[pl.BlockSpec(memory_space=pltpu.VMEM)] * 3,
        out_specs=pl.BlockSpec(memory_space=pltpu.VMEM),
        scratch_shapes=[
            pltpu.VMEM((32, rows * cols), BF16),
            pltpu.VMEM((rows, cols, 128), F32),
            pltpu.VMEM((rows, cols, 128), F32),
        ],
    )(forecast.reshape(members, rows * cols), cell_layer, coords)


def mm(a, b):
    return jnp.dot(a, b, precision=HIGHEST, preferred_element_type=F32)


def mm_tn(a, b):
    return lax.dot_general(a, b, (((0,), (0,)), ((), ())), precision=HIGHEST, preferred_element_type=F32)


def inverse_factor(block):
    size = block.shape[0]
    row = lax.broadcasted_iota(jnp.int32, (size, 2 * size), 0)
    col = lax.broadcasted_iota(jnp.int32, (size, 2 * size), 1)
    work = jnp.concatenate([block, jnp.zeros_like(block)], axis=1)
    work = jnp.where(col == row + size, 1.0, work)
    for k in range(size - 1):
        pivot = work[k : k + 1, k : k + 1]
        factor = jnp.where(row[:, 0:1] > k, work[:, k : k + 1] / pivot, 0.0)
        work = work - factor * work[k : k + 1, :]
    diagonal = jnp.sum(jnp.where(col == row, work, 0.0), axis=1, keepdims=True)
    return work[:, size:] * lax.rsqrt(diagonal)


def transform_kernel(g_ref, m_ref):
    members = g_ref.shape[0]
    size = members // 3
    row = lax.broadcasted_iota(jnp.int32, (members, members), 0)
    col = lax.broadcasted_iota(jnp.int32, (members, members), 1)
    gram = g_ref[:, 0:members] + jnp.where(row == col, members - 1.0, 0.0)
    rhs = g_ref[:, members : members + 1]
    l0 = inverse_factor(gram[0:size, 0:size])
    t0 = mm(l0, gram[0:size, size:])
    s1 = gram[size:, size:] - mm_tn(t0, t0)
    z1 = -mm_tn(t0, l0)
    l1 = inverse_factor(s1[0:size, 0:size])
    t1 = mm(l1, s1[0:size, size:])
    l10 = mm(l1, z1[0:size])
    s2 = s1[size:, size:] - mm_tn(t1, t1)
    z2 = jnp.concatenate([z1[size:] - mm_tn(t1, l10), -mm_tn(t1, l1)], axis=1)
    l2 = inverse_factor(s2)
    l20 = mm(l2, z2)
    zero = jnp.zeros((size, size), F32)
    inverse = jnp.concatenate(
        [
            jnp.concatenate([l0, zero, zero], axis=1),
            jnp.concatenate([l10, l1, zero], axis=1),
            jnp.concatenate([l20, l2], axis=1),
        ],
        axis=0,
    )
    reduced = mm(inverse, rhs)
    weights = jnp.sum(inverse * reduced, axis=0, keepdims=True)
    m_ref[...] = weights + math.sqrt(members - 1.0) * inverse


def transform(gram):
    members = gram.shape[0]
    return pl.pallas_call(
        transform_kernel,
        name="transform",
        out_shape=jax.ShapeDtypeStruct((members, members), F32),
        in_specs=[pl.BlockSpec(memory_space=pltpu.VMEM)],
        out_specs=pl.BlockSpec(memory_space=pltpu.VMEM),
    )(gram)


def shards(
    fluid_head_start,
    conductivity_matrix,
    well_rates,
    cell_layer,
    pixel_coords,
    obs_index,
    obs_value,
    obs_sigma,
):
    local_members, slab_rows, across_cells = fluid_head_start.shape
    member_count = lax.axis_size("member")
    slab_count = lax.axis_size("slab")
    slab_index = lax.axis_index("slab")
    member_index = lax.axis_index("member")
    total_rows = slab_rows * slab_count
    members = local_members * member_count
    static = jnp.concatenate([conductivity_matrix, well_rates[None]], 0)
    static_ext = padded(static, (("slab", 1),), STEPS)
    grid = padded(fluid_head_start, (("slab", 1),), STEPS)
    open_faces = face_mask(slab_index * slab_rows - STEPS, slab_rows + 2 * STEPS, total_rows)
    for repeat in range(STEPS):
        grid = advance_in_time(grid, static_ext[:-1], static_ext[-1], open_faces)
    forecast = grid[:, STEPS : STEPS + slab_rows]
    collected = lax.all_to_all(forecast, "member", split_axis=1, concat_axis=0, tiled=True)
    pile = collected.reshape(members, -1)

    pixels = pixel_coords.shape[1]
    own = pixels // (member_count * slab_count)
    shape = (-1, member_count, slab_count, own)
    coords = pixel_coords.reshape(shape).transpose(0, 2, 1, 3).reshape(-1, pixels)
    partial = subsidence_partial(forecast, cell_layer, coords, total_rows)[:local_members]
    chunk = pixels // slab_count
    partial = partial.reshape(local_members, slab_count, chunk).transpose(1, 0, 2)
    mine = lax.psum_scatter(partial, "slab", scatter_dimension=0, tiled=True)[0]
    predicted = lax.all_gather(mine, "member", axis=0, tiled=True)
    own_part = lax.dynamic_slice_in_dim(predicted, member_index * own, own, 1).T

    position = jnp.arange(chunk, dtype=jnp.int32)
    pixel = (position // own * slab_count + slab_index) * own + position % own
    hit = obs_index[:, None] == pixel[None, :]
    inverse_var = 1.0 / (obs_sigma * obs_sigma)
    sums = jnp.dot(
        jnp.stack([inverse_var, inverse_var * obs_value]), hit.astype(F32), precision=HIGHEST
    )
    centre = jnp.mean(predicted, axis=0)
    anomaly = predicted - centre[None]
    weighted = jnp.concatenate([anomaly * sums[0:1], (sums[1] - sums[0] * centre)[None]], 0)
    gram = lax.dot_general(anomaly, weighted, (((1,), (1,)), ((), ())), precision=HIGHEST)
    mix = transform(lax.psum(gram, "slab"))

    centre = jnp.mean(pile, axis=0)
    analysed = centre[None] + jnp.dot(mix, pile - centre[None], precision=HIGHEST)
    analysed = analysed.reshape(collected.shape)
    returned = lax.all_to_all(analysed, "member", split_axis=0, concat_axis=1, tiled=True)
    return (returned, own_part)


def solution(mesh):
    return jax.shard_map(
        shards,
        mesh=mesh,
        in_specs=(
            P("member", "slab", None),
            P("member", "slab", None),
            P("slab", None),
            P("slab", None),
            P(),
            P(),
            P(),
            P(),
        ),
        out_specs=(P("member", "slab", None), P(("member", "slab"), None)),
        check_vma=False,
    )
```

```python
import math

import jax
import jax.numpy as jnp
from jax import lax
from jax.experimental import pallas as pl
from jax.experimental.pallas import tpu as pltpu
from jax.sharding import PartitionSpec as P

STEPS = 4
time_step = 0.15
pixel_span = 64.0
top_depth = 2.0
F32 = jnp.float32
BF16 = jnp.bfloat16
HIGHEST = lax.Precision.HIGHEST
MESH = pl.DeviceIdType.MESH
BLOCK = 256
LANES = 128
EARLY = 10


def split(value):
    high = value.astype(BF16)
    return high, (value - high.astype(F32)).astype(BF16)


def twice(value):
    return jnp.concatenate([value, value], axis=1)


def dot(a, b, dims):
    return lax.dot_general(a, b, (dims, ((), ())), precision=HIGHEST, preferred_element_type=F32)


def mm(a, b):
    return dot(a, b, ((1,), (0,)))


def mm_tn(a, b):
    return dot(a, b, ((0,), (0,)))


def mm_nt(a, b):
    return dot(a, b, ((1,), (1,)))


def inverse_factor(block):
    size = block.shape[0]
    row = lax.broadcasted_iota(jnp.int32, (size, 2 * size), 0)
    col = lax.broadcasted_iota(jnp.int32, (size, 2 * size), 1)
    work = jnp.concatenate([block, jnp.zeros_like(block)], axis=1)
    work = jnp.where(col == row + size, 1.0, work)
    for k in range(size - 1):
        line = work[k : k + 1, :]
        scaled = line * (1.0 / work[k : k + 1, k : k + 1])
        factor = jnp.where(row[:, 0:1] > k, work[:, k : k + 1], 0.0)
        work = work - factor * scaled
    diagonal = jnp.sum(jnp.where(col == row, work, 0.0), axis=1, keepdims=True)
    return work[:, size:] * lax.rsqrt(diagonal)


def transform(packed, rhs, members):
    size = members // 3
    row = lax.broadcasted_iota(jnp.int32, (members, 2 * size), 0)
    col = lax.broadcasted_iota(jnp.int32, (members, 2 * size), 1)
    gram = packed + jnp.where(row == col, members - 1.0, 0.0)
    corner = packed[0:size, size:] + jnp.where(row == col, members - 1.0, 0.0)[0:size, 0:size]
    l0 = inverse_factor(gram[0:size, 0:size])
    t0 = mm_nt(l0, gram[size:, 0:size])
    s1 = gram[size:, size:] - mm_tn(t0, t0[:, 0:size])
    z1 = -mm_tn(t0, l0)
    l1 = inverse_factor(s1[0:size])
    t1 = mm_nt(l1, s1[size:])
    l10 = mm(l1, z1[0:size])
    s2 = corner - mm_tn(t0[:, size:], t0[:, size:]) - mm_tn(t1, t1)
    z2 = jnp.concatenate([z1[size:] - mm_tn(t1, l10), -mm_tn(t1, l1)], axis=1)
    l2 = inverse_factor(s2)
    l20 = mm(l2, z2)
    zero = jnp.zeros((size, size), F32)
    inverse = jnp.concatenate(
        [
            jnp.concatenate([l0, zero, zero], axis=1),
            jnp.concatenate([l10, l1, zero], axis=1),
            jnp.concatenate([l20, l2], axis=1),
        ],
        axis=0,
    )
    reduced = jnp.sum(inverse * rhs, axis=1, keepdims=True)
    weights = jnp.sum(inverse * reduced, axis=0, keepdims=True)
    return weights + math.sqrt(members - 1.0) * inverse


def advance(head, perm, source, open_first, open_last, first_row, rows):
    mobility = perm * (1.0 + 0.5 * jnp.tanh(head))
    last = head.shape[0] - 1
    cols = head.shape[2]
    flux = 0.5 * (mobility[1:] + mobility[:-1]) * (head[1:] - head[:-1])
    parts = [flux[i : i + 1] for i in range(last)]
    near, far = STEPS - 1 - first_row, STEPS - 1 + rows - first_row
    parts[near] = parts[near] * open_first
    parts[far] = parts[far] * open_last
    flux = jnp.concatenate(parts, axis=0)
    inner = head[1:-1]
    own = mobility[1:-1]
    lane = lax.broadcasted_iota(jnp.int32, inner.shape, 2)
    along = 0.5 * (jnp.roll(own, -1, axis=2) + own) * (jnp.roll(inner, -1, axis=2) - inner)
    along = jnp.where(lane < cols - 1, along, 0.0)
    back = jnp.where(lane > 0, jnp.roll(along, 1, axis=2), 0.0)
    inflow = (flux[1:] - flux[:-1]) + (along - back)
    return inner + time_step * (inflow + source[1:-1])


def cycle_kernel(
    total_rows,
    head_ref,
    cond_ref,
    well_ref,
    lay_ref,
    pc_ref,
    oi_ref,
    ov_ref,
    os_ref,
    ret_ref,
    own_ref,
    hx,
    cx,
    wx,
    fore,
    w_ref,
    h2_ref,
    vh_ref,
    khi,
    klo,
    part,
    rs,
    mine,
    ag,
    flat,
    turned,
    gpart,
    gred,
    gall,
    pile,
    snd,
    back,
    halo_s,
    halo_r,
    out_s,
    out_r,
    rs_s,
    rs_r,
    ag_s,
    ag_r,
    g1_s,
    g1_r,
    g2_s,
    g2_r,
    rt_s,
    rt_r,
):
    slab, member = lax.axis_index("slab"), lax.axis_index("member")
    slabs, groups = lax.axis_size("slab"), lax.axis_size("member")
    rows, local, cols = head_ref.shape
    members = local * groups
    blocks = pc_ref.shape[1] // BLOCK
    row_pitch, col_pitch = pixel_span / total_rows, pixel_span / cols
    volume = pixel_span * pixel_span / (total_rows * cols)

    def other(i, axis):
        me, n = (slab, slabs) if axis == "slab" else (member, groups)
        return lax.rem(me + i, n)

    def peers(axis, body):
        n = slabs if axis == "slab" else groups

        def step(i, carry):
            body(other(i, axis))
            return carry

        lax.fori_loop(1, n, step, 0)

    def copy(src, dst, ssem, rsem, axis, to):
        return pltpu.make_async_remote_copy(
            src_ref=src,
            dst_ref=dst,
            send_sem=ssem,
            recv_sem=rsem,
            device_id={axis: to},
            device_id_type=MESH,
        )

    barrier = pltpu.get_barrier_semaphore()
    for axis in ("slab", "member"):
        peers(
            axis,
            lambda to: pl.semaphore_signal(barrier, inc=1, device_id={axis: to}, device_id_type=MESH),
        )

    depth = top_depth + lay_ref[...].astype(F32)
    depth = jnp.concatenate([depth, jnp.zeros((cols - rows, cols), F32)], axis=0).T
    for i in range(rows):
        column = depth[:, i : i + 1]
        h2_ref[i] = jnp.broadcast_to(column * column, (cols, LANES))
        vh_ref[i] = jnp.broadcast_to(volume * column, (cols, LANES))
    cell_y = (lax.broadcasted_iota(jnp.int32, (cols, BLOCK), 0).astype(F32) + 0.5) * col_pitch
    first = (slab * rows).astype(F32)

    def evaluate(b, carry):
        at = pl.multiple_of(b * BLOCK, BLOCK)
        coords = pc_ref[:, pl.ds(at, BLOCK)].astype(F32)
        delta_y = cell_y - coords[1:2]
        dy2 = delta_y * delta_y
        for i in range(rows):
            delta_x = (first + (i + 0.5)) * row_pitch - coords[0:1]
            radius = (dy2 + delta_x * delta_x) + twice(h2_ref[i])
            inv = lax.rsqrt(radius)
            high, low = split(twice(vh_ref[i]) * (inv * inv * inv))
            khi[b, cols * i : cols * i + cols, :] = high
            klo[b, cols * i : cols * i + cols, :] = low
        return carry

    early = min(EARLY, blocks - 1)
    lax.fori_loop(0, early, evaluate, 0)

    pl.semaphore_wait(barrier, slabs - 1 + groups - 1)

    up, down = other(1, "slab"), other(slabs - 1, "slab")
    halos = []
    for n, (src, dst) in enumerate(((head_ref, hx), (cond_ref, cx), (well_ref, wx))):
        halos.append(
            copy(
                src.at[pl.ds(rows - STEPS, STEPS)],
                dst.at[pl.ds(0, STEPS)],
                halo_s.at[2 * n],
                halo_r.at[2 * n],
                "slab",
                up,
            )
        )
        halos.append(
            copy(
                src.at[pl.ds(0, STEPS)],
                dst.at[pl.ds(rows + STEPS, STEPS)],
                halo_s.at[2 * n + 1],
                halo_r.at[2 * n + 1],
                "slab",
                down,
            )
        )
    for item in halos:
        item.start()
    hx[STEPS : STEPS + rows] = head_ref[...]
    cx[STEPS : STEPS + rows] = cond_ref[...]
    wx[STEPS : STEPS + rows] = well_ref[...]
    lax.fori_loop(early, blocks, evaluate, 0)

    position = lax.broadcasted_iota(jnp.int32, (LANES, oi_ref.shape[1]), 0)
    own = LANES // groups
    pixel = ((position // own) * slabs + slab) * own + lax.rem(position, own)
    hit = jnp.where(oi_ref[...] == pixel, 1.0, 0.0)
    inverse_var = 1.0 / (os_ref[...] * os_ref[...])
    first_line = lax.broadcasted_iota(jnp.int32, (8, oi_ref.shape[1]), 0) == 0
    sums = mm_nt(jnp.where(first_line, inverse_var, inverse_var * ov_ref[...]), hit)

    for item in halos:
        item.wait_recv()
    head, perm, source = hx[...], cx[...], wx[...]
    open_first = jnp.where(slab == 0, 0.0, 1.0)
    open_last = jnp.where(slab == slabs - 1, 0.0, 1.0)
    for k in range(STEPS):
        head = advance(head, perm, source, open_first, open_last, k, rows)
        perm, source = perm[1:-1], source[1:-1]
    fore[...] = head
    w_ref[...] = jnp.zeros_like(w_ref)
    for i in range(rows):
        high, low = split(head[i])
        w_ref[0:local, cols * i : cols * i + cols] = high
        w_ref[16 : 16 + local, cols * i : cols * i + cols] = low

    peers(
        "member",
        lambda to: copy(
            fore.at[to], pile.at[member], out_s.at[to], out_r.at[member], "member", to
        ).start(),
    )

    def product(n, carry):
        b = lax.rem(n + slab // 2, blocks)
        total = jnp.dot(w_ref[...], khi[b], preferred_element_type=F32)
        total += jnp.dot(w_ref[...], klo[b], preferred_element_type=F32)
        total = total[0:16] + total[16:32]
        for half in range(BLOCK // LANES):
            to = b * (BLOCK // LANES) + half
            part[to] = total[0:local, LANES * half : LANES * half + LANES]

            @pl.when(to != slab)
            def _():
                copy(part.at[to], rs.at[slab], rs_s.at[to], rs_r.at[slab], "slab", to).start()

        return carry

    lax.fori_loop(0, blocks, product, 0)

    def rs_wait(frm):
        copy(part.at[frm], rs.at[frm], rs_s.at[frm], rs_r.at[frm], "slab", frm).wait_recv()

    peers("slab", rs_wait)
    rs[slab] = part[slab]
    total = rs[0]
    for n in range(1, slabs):
        total += rs[n]
    ag[member] = total
    mine[...] = total
    peers(
        "member",
        lambda to: copy(mine, ag.at[member], ag_s.at[to], ag_r.at[member], "member", to).start(),
    )
    peers(
        "member",
        lambda frm: copy(mine, ag.at[frm], ag_s.at[frm], ag_r.at[frm], "member", frm).wait_recv(),
    )
    for n in range(groups):
        flat[local * n : local * n + local, :] = ag[n]
    predicted = flat[...]
    centre = jnp.sum(predicted, axis=0, keepdims=True) * (1.0 / members)
    anomaly = predicted - centre
    counts = sums[0:1]
    gram = mm_nt(anomaly, anomaly * counts)
    rhs = mm_nt(jnp.broadcast_to(sums[1:2] - counts * centre, (8, LANES)), anomaly)
    size = members // 3
    top = jnp.concatenate([gram[0:size, 0:size], gram[2 * size :, 2 * size :]], axis=1)
    pieces = [top, gram[size:, 0 : 2 * size], rhs[:, 0:LANES]]
    pieces.append(jnp.concatenate([rhs[:, LANES:], jnp.zeros((8, 2 * LANES - members), F32)], axis=1))
    height = gpart.shape[1]
    pieces.append(jnp.zeros((slabs * height - members - 16, LANES), F32))
    gpart[...] = jnp.concatenate(pieces, axis=0).reshape(slabs, height, LANES)
    peers(
        "slab",
        lambda to: copy(
            gpart.at[to], gred.at[slab], g1_s.at[to], g1_r.at[slab], "slab", to
        ).start(),
    )
    predicted = jnp.concatenate([predicted, jnp.zeros((2 * LANES - members, LANES), F32)], axis=0)
    turned[...] = predicted.T
    own_ref[...] = turned[pl.ds(pl.multiple_of(member * own, own), own), :][:, 0:members]
    peers(
        "slab",
        lambda frm: copy(
            gpart.at[frm], gred.at[frm], g1_s.at[frm], g1_r.at[frm], "slab", frm
        ).wait_recv(),
    )
    gred[slab] = gpart[slab]
    total = gred[0]
    for n in range(1, slabs):
        total += gred[n]
    gall[slab] = total
    peers(
        "slab",
        lambda to: copy(
            gall.at[slab], gall.at[slab], g2_s.at[to], g2_r.at[slab], "slab", to
        ).start(),
    )
    peers(
        "member",
        lambda frm: copy(
            fore.at[frm], pile.at[frm], out_s.at[frm], out_r.at[frm], "member", frm
        ).wait_recv(),
    )
    pile[member] = fore[member]
    for n in range(groups):
        flat[local * n : local * n + local, :] = pile[n]
    spread = flat[...]
    centre = jnp.sum(spread, axis=0, keepdims=True) * (1.0 / members)
    spread = spread - centre
    peers(
        "slab",
        lambda frm: copy(
            gall.at[frm], gall.at[frm], g2_s.at[frm], g2_r.at[frm], "slab", frm
        ).wait_recv(),
    )
    packed = gall[...].reshape(slabs * height, LANES)
    rhs = jnp.concatenate(
        [packed[members : members + 1], packed[members + 8 : members + 9]], axis=1
    )[:, 0:members]
    mix = transform(packed[0:members], rhs, members)
    flat[...] = centre + mm(mix, spread)
    for n in range(groups):
        snd[n] = flat[local * n : local * n + local, :]
    peers(
        "member",
        lambda to: copy(
            snd.at[to], back.at[member], rt_s.at[to], rt_r.at[member], "member", to
        ).start(),
    )
    back[member] = snd[member]
    peers(
        "member",
        lambda frm: copy(
            snd.at[frm], back.at[frm], rt_s.at[frm], rt_r.at[frm], "member", frm
        ).wait_recv(),
    )
    ret_ref[...] = back[...]

    for item in halos:
        item.wait_send()

    def drain_member(to):
        copy(fore.at[to], pile.at[to], out_s.at[to], out_r.at[to], "member", to).wait_send()
        copy(mine, ag.at[to], ag_s.at[to], ag_r.at[to], "member", to).wait_send()
        copy(snd.at[to], back.at[to], rt_s.at[to], rt_r.at[to], "member", to).wait_send()

    def drain_slab(to):
        copy(part.at[to], rs.at[to], rs_s.at[to], rs_r.at[to], "slab", to).wait_send()
        copy(gpart.at[to], gred.at[to], g1_s.at[to], g1_r.at[to], "slab", to).wait_send()
        copy(gall.at[slab], gall.at[to], g2_s.at[to], g2_r.at[to], "slab", to).wait_send()

    peers("member", drain_member)
    peers("slab", drain_slab)


def shards(
    fluid_head_start,
    conductivity_matrix,
    well_rates,
    cell_layer,
    pixel_coords,
    obs_index,
    obs_value,
    obs_sigma,
):
    local, rows, cols = fluid_head_start.shape
    groups = lax.axis_size("member")
    slabs = lax.axis_size("slab")
    members = local * groups
    pixels = pixel_coords.shape[1]
    own = pixels // (groups * slabs)
    height = 256 // slabs
    coords = pixel_coords.reshape(-1, groups, slabs, own).transpose(0, 2, 1, 3).reshape(-1, pixels)
    vmem = pl.BlockSpec(memory_space=pltpu.VMEM)
    dma = pltpu.SemaphoreType.DMA
    tall = rows + 2 * STEPS
    blocks = pixels // BLOCK
    body = lambda *refs: cycle_kernel(rows * slabs, *refs)
    returned, own_part = pl.pallas_call(
        body,
        name="cycle",
        out_shape=(
            jax.ShapeDtypeStruct((groups, local, cols), F32),
            jax.ShapeDtypeStruct((own, members), F32),
        ),
        in_specs=[vmem] * 8,
        out_specs=(vmem, vmem),
        scratch_shapes=[
            pltpu.VMEM((tall, local, cols), F32),
            pltpu.VMEM((tall, local, cols), F32),
            pltpu.VMEM((tall, 1, cols), F32),
            pltpu.VMEM((rows, local, cols), F32),
            pltpu.VMEM((32, rows * cols), BF16),
            pltpu.VMEM((rows, cols, LANES), F32),
            pltpu.VMEM((rows, cols, LANES), F32),
            pltpu.VMEM((blocks, rows * cols, BLOCK), BF16),
            pltpu.VMEM((blocks, rows * cols, BLOCK), BF16),
            pltpu.VMEM((slabs, local, LANES), F32),
            pltpu.VMEM((slabs, local, LANES), F32),
            pltpu.VMEM((local, LANES), F32),
            pltpu.VMEM((groups, local, LANES), F32),
            pltpu.VMEM((members, LANES), F32),
            pltpu.VMEM((LANES, 2 * LANES), F32),
            pltpu.VMEM((slabs, height, LANES), F32),
            pltpu.VMEM((slabs, height, LANES), F32),
            pltpu.VMEM((slabs, height, LANES), F32),
            pltpu.VMEM((groups, local, cols), F32),
            pltpu.VMEM((groups, local, cols), F32),
            pltpu.VMEM((groups, local, cols), F32),
            dma((6,)),
            dma((6,)),
            dma((groups,)),
            dma((groups,)),
            dma((slabs,)),
            dma((slabs,)),
            dma((groups,)),
            dma((groups,)),
            dma((slabs,)),
            dma((slabs,)),
            dma((slabs,)),
            dma((slabs,)),
            dma((groups,)),
            dma((groups,)),
        ],
        compiler_params=pltpu.CompilerParams(
            collective_id=0, has_side_effects=True, vmem_limit_bytes=60 * 1024 * 1024
        ),
    )(
        fluid_head_start.transpose(1, 0, 2),
        conductivity_matrix.transpose(1, 0, 2),
        well_rates[:, None, :],
        cell_layer,
        coords,
        obs_index[None],
        obs_value[None],
        obs_sigma[None],
    )
    return (returned.transpose(1, 0, 2), own_part)


def solution(mesh):
    return jax.shard_map(
        shards,
        mesh=mesh,
        in_specs=(
            P("member", "slab", None),
            P("member", "slab", None),
            P("slab", None),
            P("slab", None),
            P(),
            P(),
            P(),
            P(),
        ),
        out_specs=(P("member", "slab", None), P(("member", "slab"), None)),
        check_vma=False,
    )
```

```python
import math

import jax
import jax.numpy as jnp
from jax import lax
from jax.experimental import pallas as pl
from jax.experimental.pallas import tpu as pltpu
from jax.sharding import PartitionSpec as P

STEPS = 4
time_step = 0.15
pixel_span = 64.0
top_depth = 2.0
F32 = jnp.float32
BF16 = jnp.bfloat16
HIGHEST = lax.Precision.HIGHEST
MESH = pl.DeviceIdType.MESH
BLOCK = 256
LANES = 128
EARLY = 8
MIDDLE = 14
FIRST = 9


def split(value):
    high = value.astype(BF16)
    return high, (value - high.astype(F32)).astype(BF16)


def twice(value):
    return jnp.concatenate([value, value], axis=1)


def dot(a, b, dims):
    return lax.dot_general(a, b, (dims, ((), ())), precision=HIGHEST, preferred_element_type=F32)


def mm(a, b):
    return dot(a, b, ((1,), (0,)))


def mm_tn(a, b):
    return dot(a, b, ((0,), (0,)))


def mm_nt(a, b):
    return dot(a, b, ((1,), (1,)))


def inverse_factor(block):
    size = block.shape[0]
    wide = 2 * size
    count = size // 8
    sub = lax.broadcasted_iota(jnp.int32, (8, wide), 0)
    lane = lax.broadcasted_iota(jnp.int32, (8, wide), 1)

    def full(value):
        return jnp.broadcast_to(value, (8, wide))

    tiles = []
    for t in range(count):
        unit = jnp.where(lane == sub + (8 * t + size), 1.0, 0.0)
        tiles.append(jnp.concatenate([block[8 * t : 8 * t + 8], unit[:, size:]], axis=1))
    out = []
    for q in range(count):
        start = 8 * q
        cols = [
            [full(tiles[t][:, start + j : start + j + 1]) for t in range(q, count)] for j in range(8)
        ]
        lines = []
        top = tiles[q]
        pivots = None
        for k in range(8):
            mine = cols[k]
            pivot = full(mine[0][k : k + 1, :])
            pivots = pivot if k == 0 else jnp.where(sub == k, pivot, pivots)
            inv = 1.0 / pivot
            for j in range(k + 1, 8):
                ratio = full(mine[0][j : j + 1, :]) * inv
                cols[j] = [c - m * ratio for c, m in zip(cols[j], mine)]
            line = full(top[k : k + 1, :]) * inv
            lines.append(line)
            if k < 7:
                top = top - jnp.where(sub > k, mine[0], 0.0) * line
        out.append(top[:, size:] * lax.rsqrt(pivots)[:, size:])
        for t in range(q + 1, count):
            for k in range(8):
                tiles[t] = tiles[t] - cols[k][t - q] * lines[k]
    return jnp.concatenate(out, axis=0)


def transform(packed, rhs, members):
    size = members // 3
    row = lax.broadcasted_iota(jnp.int32, (members, 2 * size), 0)
    col = lax.broadcasted_iota(jnp.int32, (members, 2 * size), 1)
    gram = packed + jnp.where(row == col, members - 1.0, 0.0)
    corner = packed[0:size, size:] + jnp.where(row == col, members - 1.0, 0.0)[0:size, 0:size]
    l0 = inverse_factor(gram[0:size, 0:size])
    t0 = mm_nt(l0, gram[size:, 0:size])
    s1 = gram[size:, size:] - mm_tn(t0, t0[:, 0:size])
    z1 = -mm_tn(t0, l0)
    l1 = inverse_factor(s1[0:size])
    t1 = mm_nt(l1, s1[size:])
    l10 = mm(l1, z1[0:size])
    s2 = corner - mm_tn(t0[:, size:], t0[:, size:]) - mm_tn(t1, t1)
    z2 = jnp.concatenate([z1[size:] - mm_tn(t1, l10), -mm_tn(t1, l1)], axis=1)
    l2 = inverse_factor(s2)
    l20 = mm(l2, z2)
    zero = jnp.zeros((size, size), F32)
    inverse = jnp.concatenate(
        [
            jnp.concatenate([l0, zero, zero], axis=1),
            jnp.concatenate([l10, l1, zero], axis=1),
            jnp.concatenate([l20, l2], axis=1),
        ],
        axis=0,
    )
    reduced = jnp.sum(inverse * rhs, axis=1, keepdims=True)
    weights = jnp.sum(inverse * reduced, axis=0, keepdims=True)
    return weights + math.sqrt(members - 1.0) * inverse


def advance(head, perm, source, open_first, open_last, first_row, rows):
    mobility = perm * (1.0 + 0.5 * jnp.tanh(head))
    last = head.shape[0] - 1
    cols = head.shape[2]
    flux = 0.5 * (mobility[1:] + mobility[:-1]) * (head[1:] - head[:-1])
    parts = [flux[i : i + 1] for i in range(last)]
    near, far = STEPS - 1 - first_row, STEPS - 1 + rows - first_row
    parts[near] = parts[near] * open_first
    parts[far] = parts[far] * open_last
    flux = jnp.concatenate(parts, axis=0)
    inner = head[1:-1]
    own = mobility[1:-1]
    lane = lax.broadcasted_iota(jnp.int32, inner.shape, 2)
    along = 0.5 * (jnp.roll(own, -1, axis=2) + own) * (jnp.roll(inner, -1, axis=2) - inner)
    along = jnp.where(lane < cols - 1, along, 0.0)
    back = jnp.where(lane > 0, jnp.roll(along, 1, axis=2), 0.0)
    inflow = (flux[1:] - flux[:-1]) + (along - back)
    return inner + time_step * (inflow + source[1:-1])


def cycle_kernel(total_rows, *refs):
    head_ref, cond_ref, well_ref, lay_ref, pc_ref, oi_ref, ov_ref, os_ref = refs[:8]
    ret_ref, own_ref = refs[8:10]
    hx, cx, wx, fore, w_ref, h2_ref, vh_ref, khi, klo, ohi, olo, place, where = refs[10:23]
    po, ro, mine, ao, flat, part, rs, turned, got, gpart, gred, gall, pile, snd, back = refs[23:38]
    halo_s, halo_r, out_s, out_r, ro_s, ro_r, ao_s, ao_r = refs[38:46]
    g1_s, g1_r, rs_s, rs_r, g2_s, g2_r, tu_s, tu_r, rt_s, rt_r = refs[46:]

    slab, member = lax.axis_index("slab"), lax.axis_index("member")
    slabs, groups = lax.axis_size("slab"), lax.axis_size("member")
    rows, local, cols = head_ref.shape
    members = local * groups
    pixels = pc_ref.shape[1]
    observed = oi_ref.shape[1]
    blocks, obs_blocks = pixels // BLOCK, observed // BLOCK
    row_pitch, col_pitch = pixel_span / total_rows, pixel_span / cols
    volume = pixel_span * pixel_span / (total_rows * cols)

    def other(i, axis):
        me, n = (slab, slabs) if axis == "slab" else (member, groups)
        return lax.rem(me + i, n)

    def peers(axis, body):
        n = slabs if axis == "slab" else groups

        def step(i, carry):
            body(other(i, axis))
            return carry

        lax.fori_loop(1, n, step, 0)

    def copy(src, dst, ssem, rsem, axis, to):
        return pltpu.make_async_remote_copy(
            src_ref=src,
            dst_ref=dst,
            send_sem=ssem,
            recv_sem=rsem,
            device_id={axis: to},
            device_id_type=MESH,
        )

    class Exchange:
        def __init__(self, axis, src, dst, ssem, rsem):
            self.axis, self.src, self.dst, self.ssem, self.rsem = axis, src, dst, ssem, rsem
            self.me = slab if axis == "slab" else member

        def make(self, to, at):
            return copy(
                self.src(to), self.dst.at[at], self.ssem.at[to], self.rsem.at[at], self.axis, to
            )

        def start(self):
            peers(self.axis, lambda to: self.make(to, self.me).start())

        def arrive(self):
            peers(self.axis, lambda frm: self.make(frm, frm).wait_recv())

        def drain(self):
            peers(self.axis, lambda to: self.make(to, to).wait_send())

    def total_of(ref):
        value = ref[0]
        for n in range(1, ref.shape[0]):
            value += ref[n]
        return value

    send_fore = Exchange("member", lambda to: fore.at[to], pile, out_s, out_r)
    send_obs = Exchange("slab", lambda to: po.at[to], ro, ro_s, ro_r)
    send_mine = Exchange("member", lambda to: mine, ao, ao_s, ao_r)
    send_gram = Exchange("slab", lambda to: gpart.at[to], gred, g1_s, g1_r)
    send_part = Exchange("slab", lambda to: part.at[to], rs, rs_s, rs_r)
    send_sum = Exchange("slab", lambda to: gall.at[slab], gall, g2_s, g2_r)
    send_own = Exchange("member", lambda to: turned.at[to], got, tu_s, tu_r)
    send_back = Exchange("member", lambda to: snd.at[to], back, rt_s, rt_r)

    barrier = pltpu.get_barrier_semaphore()
    for axis in ("slab", "member"):
        peers(
            axis,
            lambda to: pl.semaphore_signal(barrier, inc=1, device_id={axis: to}, device_id_type=MESH),
        )

    depth = top_depth + lay_ref[...].astype(F32)
    depth = jnp.concatenate([depth, jnp.zeros((cols - rows, cols), F32)], axis=0).T
    for i in range(rows):
        column = depth[:, i : i + 1]
        h2_ref[i] = jnp.broadcast_to(column * column, (cols, LANES))
        vh_ref[i] = jnp.broadcast_to(volume * column, (cols, LANES))
    cell_y = (lax.broadcasted_iota(jnp.int32, (cols, BLOCK), 0).astype(F32) + 0.5) * col_pitch
    first = (slab * rows).astype(F32)

    def evaluate(coords_ref, high_ref, low_ref):
        def step(b, carry):
            at = pl.multiple_of(b * BLOCK, BLOCK)
            coords = coords_ref[0:2, pl.ds(at, BLOCK)].astype(F32)
            delta_y = cell_y - coords[1:2]
            dy2 = delta_y * delta_y
            for i in range(rows):
                delta_x = (first + (i + 0.5)) * row_pitch - coords[0:1]
                radius = (dy2 + delta_x * delta_x) + twice(h2_ref[i])
                inv = lax.rsqrt(radius)
                high, low = split(twice(vh_ref[i]) * (inv * inv * inv))
                high_ref[b, cols * i : cols * i + cols, :] = high
                low_ref[b, cols * i : cols * i + cols, :] = low
            return carry

        return step

    groups_of = pixels // LANES
    for c in range(2):
        for n in range(groups_of):
            place[groups_of * c + n : groups_of * c + n + 1, :] = pc_ref[
                c : c + 1, LANES * n : LANES * n + LANES
            ].astype(F32)
    index = oi_ref[...]
    own = LANES // groups
    chosen = (index // own) // slabs
    within = lax.rem(index // own, slabs) * LANES + chosen * own + lax.rem(index, own)
    high_part, low_part = within // LANES, lax.rem(within, LANES)
    line = lax.broadcasted_iota(jnp.int32, (groups_of, observed), 0)
    pick = jnp.where(line == high_part, 1.0, 0.0).astype(BF16)
    spot = lax.broadcasted_iota(jnp.int32, (LANES, observed), 0) == low_part
    for c in range(2):
        table = place[groups_of * c : groups_of * c + groups_of, :].astype(BF16)
        near = lax.dot_general(table, pick, (((0,), (0,)), ((), ())), preferred_element_type=F32)
        where[c : c + 1, :] = jnp.sum(jnp.where(spot, near, 0.0), axis=0, keepdims=True)
    lax.fori_loop(0, obs_blocks, evaluate(where, ohi, olo), 0)
    every = evaluate(pc_ref, khi, klo)
    lax.fori_loop(0, EARLY, every, 0)

    pl.semaphore_wait(barrier, slabs - 1 + groups - 1)

    up, down = other(1, "slab"), other(slabs - 1, "slab")
    halos = []
    for n, (src, dst) in enumerate(((head_ref, hx), (cond_ref, cx), (well_ref, wx))):
        for side, (frm, at, to) in enumerate(((rows - STEPS, 0, up), (0, rows + STEPS, down))):
            halos.append(
                copy(
                    src.at[pl.ds(frm, STEPS)],
                    dst.at[pl.ds(at, STEPS)],
                    halo_s.at[2 * n + side],
                    halo_r.at[2 * n + side],
                    "slab",
                    to,
                )
            )
    for item in halos:
        item.start()
    hx[STEPS : STEPS + rows] = head_ref[...]
    cx[STEPS : STEPS + rows] = cond_ref[...]
    wx[STEPS : STEPS + rows] = well_ref[...]
    lax.fori_loop(EARLY, MIDDLE, every, 0)
    width = observed // slabs
    inverse_var = 1.0 / (os_ref[...] * os_ref[...])
    first_line = lax.broadcasted_iota(jnp.int32, (8, observed), 0) == 0
    observations = jnp.where(first_line, inverse_var, ov_ref[...])
    observations = pltpu.roll(observations, lax.rem(observed - width * slab, observed), 1)
    inside = lax.broadcasted_iota(jnp.int32, (8, LANES), 1) < width
    observations = jnp.where(inside, observations[:, 0:LANES], 0.0)

    for item in halos:
        item.wait_recv()
    head, perm, source = hx[...], cx[...], wx[...]
    open_first = jnp.where(slab == 0, 0.0, 1.0)
    open_last = jnp.where(slab == slabs - 1, 0.0, 1.0)
    for k in range(STEPS):
        head = advance(head, perm, source, open_first, open_last, k, rows)
        perm, source = perm[1:-1], source[1:-1]
    fore[...] = head
    w_ref[...] = jnp.zeros_like(w_ref)
    for i in range(rows):
        high, low = split(head[i])
        w_ref[0:local, cols * i : cols * i + cols] = high
        w_ref[16 : 16 + local, cols * i : cols * i + cols] = low

    def product(high_ref, low_ref, b):
        total = jnp.dot(w_ref[...], high_ref[b], preferred_element_type=F32)
        return total + jnp.dot(w_ref[...], low_ref[b], preferred_element_type=F32)

    shares = LANES // width
    each = local // shares
    line = lax.broadcasted_iota(jnp.int32, (32, 32), 0)
    col = lax.broadcasted_iota(jnp.int32, (32, 32), 1)
    wanted = (line // 8) * each + lax.rem(line, 8)
    valid = lax.rem(line, 8) < each
    gather = jnp.where(valid & ((col == wanted) | (col == wanted + 16)), 1.0, 0.0)
    lane = lax.broadcasted_iota(jnp.int32, (8, LANES), 1) // width
    for b in range(obs_blocks):
        total = mm(gather, product(ohi, olo, b))
        for half in range(BLOCK // LANES):
            block = total[:, LANES * half : LANES * half + LANES]
            for u in range(shares):
                chunk = None
                for g in range(shares):
                    piece = pltpu.roll(block[8 * g : 8 * g + 8], (width * (g - u)) % LANES, 1)
                    chunk = piece if g == 0 else jnp.where(lane == g, piece, chunk)
                po[(b * (BLOCK // LANES) + half) * shares + u] = chunk[0:4]
    send_obs.start()
    send_fore.start()
    ro[slab] = po[slab]

    def whole(b, carry):
        total = product(khi, klo, b)
        total = total[0:16] + total[16:32]
        for half in range(BLOCK // LANES):
            part[b * (BLOCK // LANES) + half] = total[0:local, LANES * half : LANES * half + LANES]
        return carry

    lax.fori_loop(0, FIRST, whole, 0)
    send_obs.arrive()
    total = total_of(ro)
    mine[...] = total
    ao[member] = total
    send_mine.start()
    lax.fori_loop(MIDDLE, blocks, every, 0)
    lax.fori_loop(FIRST, blocks, whole, 0)
    send_obs.drain()
    send_mine.arrive()
    lane = lax.broadcasted_iota(jnp.int32, (4, LANES), 1)
    for n in range(groups):
        tile = ao[n]
        for g in range(shares):
            piece = tile if g == 0 else pltpu.roll(tile, LANES - width * g, 1)
            at = local * n + each * g
            flat[at : at + each, :] = jnp.where(lane < width, piece, 0.0)[0:each]
    predicted = flat[...]
    centre = jnp.sum(predicted, axis=0, keepdims=True) * (1.0 / members)
    anomaly = predicted - centre
    weight = observations[0:1]
    gram = mm_nt(anomaly, anomaly * weight)
    rhs = mm_nt(jnp.broadcast_to(weight * (observations[1:2] - centre), (8, LANES)), anomaly)
    size = members // 3
    top = jnp.concatenate([gram[0:size, 0:size], gram[2 * size :, 2 * size :]], axis=1)
    pieces = [top, gram[size:, 0 : 2 * size], rhs[:, 0:LANES]]
    pieces.append(jnp.concatenate([rhs[:, LANES:], jnp.zeros((8, 2 * LANES - members), F32)], axis=1))
    height = gpart.shape[1]
    pieces.append(jnp.zeros((slabs * height - members - 16, LANES), F32))
    gpart[...] = jnp.concatenate(pieces, axis=0).reshape(slabs, height, LANES)
    send_gram.start()
    send_part.start()
    rs[slab] = part[slab]
    gred[slab] = gpart[slab]
    send_mine.drain()
    send_gram.arrive()
    gall[slab] = total_of(gred)
    send_sum.start()
    send_gram.drain()
    send_fore.arrive()
    pile[member] = fore[member]
    for n in range(groups):
        flat[local * n : local * n + local, :] = pile[n]
    spread = flat[...]
    centre = jnp.sum(spread, axis=0, keepdims=True) * (1.0 / members)
    spread = spread - centre
    send_part.arrive()
    total = jnp.concatenate([total_of(rs), jnp.zeros((LANES - local, LANES), F32)], axis=0)
    turned[...] = total.T.reshape(groups, own, LANES)
    send_sum.arrive()
    send_own.start()
    got[member] = turned[member]
    packed = gall[...].reshape(slabs * height, LANES)
    rhs = jnp.concatenate(
        [packed[members : members + 1], packed[members + 8 : members + 9]], axis=1
    )[:, 0:members]
    mix = transform(packed[0:members], rhs, members)
    flat[...] = centre + mm(mix, spread)
    for n in range(groups):
        snd[n] = flat[local * n : local * n + local, :]
    send_back.start()
    back[member] = snd[member]
    send_own.arrive()
    total = jnp.zeros((own, 2 * LANES), F32)
    for n in range(groups):
        tile = jnp.concatenate([got[n], jnp.zeros((own, LANES), F32)], axis=1)
        total += tile if n == 0 else pltpu.roll(tile, local * n, 1)
    own_ref[...] = total[:, 0:members]
    for item in halos:
        item.wait_send()
    send_fore.drain()
    send_part.drain()
    send_sum.drain()
    send_own.drain()
    send_back.arrive()
    ret_ref[...] = back[...]
    send_back.drain()


def shards(
    fluid_head_start,
    conductivity_matrix,
    well_rates,
    cell_layer,
    pixel_coords,
    obs_index,
    obs_value,
    obs_sigma,
):
    local, rows, cols = fluid_head_start.shape
    groups = lax.axis_size("member")
    slabs = lax.axis_size("slab")
    members = local * groups
    pixels = pixel_coords.shape[1]
    observed = obs_index.shape[0]
    own = pixels // (groups * slabs)
    height = 256 // slabs
    coords = pixel_coords.reshape(-1, groups, slabs, own).transpose(0, 2, 1, 3).reshape(-1, pixels)
    place = pl.BlockSpec(memory_space=pltpu.VMEM)
    tall = rows + 2 * STEPS

    def f32(*shape):
        return pltpu.VMEM(shape, F32)

    def bf16(*shape):
        return pltpu.VMEM(shape, BF16)

    def pair(n):
        return [pltpu.SemaphoreType.DMA((n,))] * 2

    body = lambda *refs: cycle_kernel(rows * slabs, *refs)
    returned, own_part = pl.pallas_call(
        body,
        name="cycle",
        out_shape=(
            jax.ShapeDtypeStruct((groups, local, cols), F32),
            jax.ShapeDtypeStruct((own, members), F32),
        ),
        in_specs=[place] * 8,
        out_specs=(place, place),
        scratch_shapes=[
            f32(tall, local, cols),
            f32(tall, local, cols),
            f32(tall, 1, cols),
            f32(rows, local, cols),
            bf16(32, rows * cols),
            f32(rows, cols, LANES),
            f32(rows, cols, LANES),
            bf16(pixels // BLOCK, rows * cols, BLOCK),
            bf16(pixels // BLOCK, rows * cols, BLOCK),
            bf16(observed // BLOCK, rows * cols, BLOCK),
            bf16(observed // BLOCK, rows * cols, BLOCK),
            f32(2 * pixels // LANES, LANES),
            f32(8, observed),
            f32(slabs, 4, LANES),
            f32(slabs, 4, LANES),
            f32(4, LANES),
            f32(groups, 4, LANES),
            f32(members, LANES),
            f32(slabs, local, LANES),
            f32(slabs, local, LANES),
            f32(groups, own, LANES),
            f32(groups, own, LANES),
            f32(slabs, height, LANES),
            f32(slabs, height, LANES),
            f32(slabs, height, LANES),
            f32(groups, local, cols),
            f32(groups, local, cols),
            f32(groups, local, cols),
            *pair(6),
            *pair(groups),
            *pair(slabs),
            *pair(groups),
            *pair(slabs),
            *pair(slabs),
            *pair(slabs),
            *pair(groups),
            *pair(groups),
        ],
        compiler_params=pltpu.CompilerParams(
            collective_id=0, has_side_effects=True, vmem_limit_bytes=60 * 1024 * 1024
        ),
    )(
        fluid_head_start.transpose(1, 0, 2),
        conductivity_matrix.transpose(1, 0, 2),
        well_rates[:, None, :],
        cell_layer,
        coords,
        obs_index[None],
        obs_value[None],
        obs_sigma[None],
    )
    return (returned.transpose(1, 0, 2), own_part)


def solution(mesh):
    return jax.shard_map(
        shards,
        mesh=mesh,
        in_specs=(
            P("member", "slab", None),
            P("member", "slab", None),
            P("slab", None),
            P("slab", None),
            P(),
            P(),
            P(),
            P(),
        ),
        out_specs=(P("member", "slab", None), P(("member", "slab"), None)),
        check_vma=False,
    )
```

```python
import math

import jax
import jax.numpy as jnp
from jax import lax
from jax.experimental import pallas as pl
from jax.experimental.pallas import tpu as pltpu
from jax.sharding import PartitionSpec as P

STEPS = 4
time_step = 0.15
pixel_span = 64.0
top_depth = 2.0
F32 = jnp.float32
BF16 = jnp.bfloat16
HIGHEST = lax.Precision.HIGHEST
MESH = pl.DeviceIdType.MESH
BLOCK = 256
LANES = 128
EARLY = 3
MIDDLE = 9
LATE = 11
FIRST = 9


def split(value):
    high = value.astype(BF16)
    return high, (value - high.astype(F32)).astype(BF16)


def twice(value):
    return jnp.concatenate([value, value], axis=1)


def dot(a, b, dims):
    return lax.dot_general(a, b, (dims, ((), ())), precision=HIGHEST, preferred_element_type=F32)


def mm(a, b):
    return dot(a, b, ((1,), (0,)))


def mm_tn(a, b):
    return dot(a, b, ((0,), (0,)))


def mm_nt(a, b):
    return dot(a, b, ((1,), (1,)))


def inverse_factor(block):
    size = block.shape[0]
    wide = 2 * size
    count = size // 8
    sub = lax.broadcasted_iota(jnp.int32, (8, wide), 0)
    lane = lax.broadcasted_iota(jnp.int32, (8, wide), 1)

    def full(value):
        return jnp.broadcast_to(value, (8, wide))

    tiles = []
    for t in range(count):
        unit = jnp.where(lane == sub + (8 * t + size), 1.0, 0.0)
        tiles.append(jnp.concatenate([block[8 * t : 8 * t + 8], unit[:, size:]], axis=1))
    out = []
    for q in range(count):
        start = 8 * q
        cols = [
            [full(tiles[t][:, start + j : start + j + 1]) for t in range(q, count)] for j in range(8)
        ]
        lines = []
        top = tiles[q]
        pivots = None
        for k in range(8):
            mine = cols[k]
            pivot = full(mine[0][k : k + 1, :])
            pivots = pivot if k == 0 else jnp.where(sub == k, pivot, pivots)
            inv = 1.0 / pivot
            for j in range(k + 1, 8):
                ratio = full(mine[0][j : j + 1, :]) * inv
                cols[j] = [c - m * ratio for c, m in zip(cols[j], mine)]
            line = full(top[k : k + 1, :]) * inv
            lines.append(line)
            if k < 7:
                top = top - jnp.where(sub > k, mine[0], 0.0) * line
        out.append(top[:, size:] * lax.rsqrt(pivots)[:, size:])
        for t in range(q + 1, count):
            for k in range(8):
                tiles[t] = tiles[t] - cols[k][t - q] * lines[k]
    return jnp.concatenate(out, axis=0)


def transform(packed, rhs, members):
    size = members // 3
    row = lax.broadcasted_iota(jnp.int32, (members, 2 * size), 0)
    col = lax.broadcasted_iota(jnp.int32, (members, 2 * size), 1)
    gram = packed + jnp.where(row == col, members - 1.0, 0.0)
    corner = packed[0:size, size:] + jnp.where(row == col, members - 1.0, 0.0)[0:size, 0:size]
    l0 = inverse_factor(gram[0:size, 0:size])
    t0 = mm_nt(l0, gram[size:, 0:size])
    s1 = gram[size:, size:] - mm_tn(t0, t0[:, 0:size])
    z1 = -mm_tn(t0, l0)
    l1 = inverse_factor(s1[0:size])
    t1 = mm_nt(l1, s1[size:])
    l10 = mm(l1, z1[0:size])
    s2 = corner - mm_tn(t0[:, size:], t0[:, size:]) - mm_tn(t1, t1)
    z2 = jnp.concatenate([z1[size:] - mm_tn(t1, l10), -mm_tn(t1, l1)], axis=1)
    l2 = inverse_factor(s2)
    l20 = mm(l2, z2)
    zero = jnp.zeros((size, size), F32)
    inverse = jnp.concatenate(
        [
            jnp.concatenate([l0, zero, zero], axis=1),
            jnp.concatenate([l10, l1, zero], axis=1),
            jnp.concatenate([l20, l2], axis=1),
        ],
        axis=0,
    )
    reduced = jnp.sum(inverse * rhs, axis=1, keepdims=True)
    weights = jnp.sum(inverse * reduced, axis=0, keepdims=True)
    return weights + math.sqrt(members - 1.0) * inverse


def advance(head, perm, source, open_first, open_last, first_row, rows):
    mobility = perm * (1.0 + 0.5 * jnp.tanh(head))
    last = head.shape[0] - 1
    cols = head.shape[2]
    flux = 0.5 * (mobility[1:] + mobility[:-1]) * (head[1:] - head[:-1])
    parts = [flux[i : i + 1] for i in range(last)]
    near, far = STEPS - 1 - first_row, STEPS - 1 + rows - first_row
    parts[near] = parts[near] * open_first
    parts[far] = parts[far] * open_last
    flux = jnp.concatenate(parts, axis=0)
    inner = head[1:-1]
    own = mobility[1:-1]
    lane = lax.broadcasted_iota(jnp.int32, inner.shape, 2)
    along = 0.5 * (jnp.roll(own, -1, axis=2) + own) * (jnp.roll(inner, -1, axis=2) - inner)
    along = jnp.where(lane < cols - 1, along, 0.0)
    back = jnp.where(lane > 0, jnp.roll(along, 1, axis=2), 0.0)
    inflow = (flux[1:] - flux[:-1]) + (along - back)
    return inner + time_step * (inflow + source[1:-1])


def cycle_kernel(total_rows, *refs):
    head_ref, cond_ref, well_ref, lay_ref, pc_ref, oi_ref, ov_ref, os_ref = refs[:8]
    ret_ref, own_ref = refs[8:10]
    hx, cx, wx, fore, w_ref, h2_ref, vh_ref, khi, klo, ohi, olo, place, where = refs[10:23]
    pcs, po, ro, mine, ao, flat, part, rs, turned, got, gpart, gred, gall, pile, snd, back = refs[23:39]
    halo_s, halo_r, out_s, out_r, ro_s, ro_r, ao_s, ao_r = refs[39:47]
    g1_s, g1_r, rs_s, rs_r, g2_s, g2_r, tu_s, tu_r, rt_s, rt_r = refs[47:]

    slab, member = lax.axis_index("slab"), lax.axis_index("member")
    slabs, groups = lax.axis_size("slab"), lax.axis_size("member")
    local, rows, cols = head_ref.shape
    members = local * groups
    pixels = pc_ref.shape[1]
    observed = oi_ref.shape[1]
    blocks, obs_blocks = pixels // BLOCK, observed // BLOCK
    row_pitch, col_pitch = pixel_span / total_rows, pixel_span / cols
    volume = pixel_span * pixel_span / (total_rows * cols)

    def other(i, axis):
        me, n = (slab, slabs) if axis == "slab" else (member, groups)
        return lax.rem(me + i, n)

    def peers(axis, body):
        n = slabs if axis == "slab" else groups

        def step(i, carry):
            body(other(i, axis))
            return carry

        lax.fori_loop(1, n, step, 0)

    def copy(src, dst, ssem, rsem, axis, to):
        return pltpu.make_async_remote_copy(
            src_ref=src,
            dst_ref=dst,
            send_sem=ssem,
            recv_sem=rsem,
            device_id={axis: to},
            device_id_type=MESH,
        )

    class Exchange:
        def __init__(self, axis, src, dst, ssem, rsem):
            self.axis, self.src, self.dst, self.ssem, self.rsem = axis, src, dst, ssem, rsem
            self.me = slab if axis == "slab" else member

        def start(self):
            def one(to):
                copy(
                    self.src(to), self.dst.at[self.me], self.ssem, self.rsem, self.axis, to
                ).start()

            peers(self.axis, one)

        def every(self):
            part = self.dst.at[pl.ds(0, self.dst.shape[0] - 1)]
            return copy(part, part, self.ssem, self.rsem, self.axis, other(1, self.axis))

        def arrive(self):
            self.every().wait_recv()

        def drain(self):
            self.every().wait_send()

    def total_of(ref):
        value = ref[0]
        for n in range(1, ref.shape[0]):
            value += ref[n]
        return value

    send_fore = Exchange("member", lambda to: fore.at[to], pile, out_s, out_r)
    send_obs = Exchange("slab", lambda to: po.at[to], ro, ro_s, ro_r)
    send_mine = Exchange("member", lambda to: mine, ao, ao_s, ao_r)
    send_gram = Exchange("slab", lambda to: gpart.at[to], gred, g1_s, g1_r)
    send_part = Exchange("slab", lambda to: part.at[to], rs, rs_s, rs_r)
    send_sum = Exchange("slab", lambda to: gall.at[slab], gall, g2_s, g2_r)
    send_own = Exchange("member", lambda to: turned.at[to], got, tu_s, tu_r)
    send_back = Exchange("member", lambda to: snd.at[to], back, rt_s, rt_r)

    barrier = pltpu.get_barrier_semaphore()
    for axis in ("slab", "member"):
        peers(
            axis,
            lambda to: pl.semaphore_signal(barrier, inc=1, device_id={axis: to}, device_id_type=MESH),
        )

    for i in range(rows):
        hx[STEPS + i] = head_ref[:, i, :]
        cx[STEPS + i] = cond_ref[:, i, :]
        wx[STEPS + i] = well_ref[i : i + 1, :]
    depth = top_depth + lay_ref[...].astype(F32)
    depth = jnp.concatenate([depth, jnp.zeros((cols - rows, cols), F32)], axis=0).T
    for i in range(rows):
        column = depth[:, i : i + 1]
        h2_ref[i] = jnp.broadcast_to(column * column, (cols, LANES))
        vh_ref[i] = jnp.broadcast_to(volume * column, (cols, LANES))
    cell_y = (lax.broadcasted_iota(jnp.int32, (cols, BLOCK), 0).astype(F32) + 0.5) * col_pitch
    first = (slab * rows).astype(F32)

    def evaluate(coords_ref, high_ref, low_ref):
        def step(b, carry):
            at = pl.multiple_of(b * BLOCK, BLOCK)
            coords = coords_ref[0:2, pl.ds(at, BLOCK)].astype(F32)
            delta_y = cell_y - coords[1:2]
            dy2 = delta_y * delta_y
            for i in range(rows):
                delta_x = (first + (i + 0.5)) * row_pitch - coords[0:1]
                radius = (dy2 + delta_x * delta_x) + twice(h2_ref[i])
                inv = lax.rsqrt(radius)
                high, low = split(twice(vh_ref[i]) * (inv * inv * inv))
                high_ref[b, cols * i : cols * i + cols, :] = high
                low_ref[b, cols * i : cols * i + cols, :] = low
            return carry

        return step

    groups_of = pixels // LANES
    for c in range(2):
        for n in range(groups_of):
            place[groups_of * c + n : groups_of * c + n + 1, :] = pc_ref[
                c : c + 1, LANES * n : LANES * n + LANES
            ].astype(F32)
    own = LANES // groups
    near = slabs * own // LANES
    line = lax.broadcasted_iota(jnp.int32, (groups, LANES), 0)
    lane = lax.broadcasted_iota(jnp.int32, (groups, LANES), 1)
    widen = jnp.where(lane // own == line, 1.0, 0.0).astype(BF16)
    line = lax.broadcasted_iota(jnp.int32, (LANES, LANES), 0)
    lane = lax.broadcasted_iota(jnp.int32, (LANES, LANES), 1)
    same = lax.rem(line, own) == lax.rem(lane, own)
    for c in range(2):
        for h in range(near):
            table = place[pl.ds(groups_of * c + h, groups, stride=near), :].astype(BF16)
            wide = lax.dot_general(
                table, widen, (((0,), (0,)), ((), ())), preferred_element_type=F32
            )
            wide = jnp.sum(jnp.where(same, wide, 0.0).reshape(LANES // own, own, LANES), axis=1)
            for n in range(LANES // own):
                at = (h * (LANES // own) + n) * LANES
                pcs[c : c + 1, at : at + LANES] = wide[n : n + 1]
    high_part, low_part = oi_ref[...] // LANES, lax.rem(oi_ref[...], LANES)
    line = lax.broadcasted_iota(jnp.int32, (groups_of, observed), 0)
    pick = jnp.where(line == high_part, 1.0, 0.0).astype(BF16)
    spot = lax.broadcasted_iota(jnp.int32, (LANES, observed), 0) == low_part
    for c in range(2):
        table = place[groups_of * c : groups_of * c + groups_of, :].astype(BF16)
        found = lax.dot_general(table, pick, (((0,), (0,)), ((), ())), preferred_element_type=F32)
        where[c : c + 1, :] = jnp.sum(jnp.where(spot, found, 0.0), axis=0, keepdims=True)
    lax.fori_loop(0, obs_blocks, evaluate(where, ohi, olo), 0)
    every = evaluate(pcs, khi, klo)
    lax.fori_loop(0, EARLY, every, 0)

    pl.semaphore_wait(barrier, slabs - 1 + groups - 1)

    up, down = other(1, "slab"), other(slabs - 1, "slab")
    halos = []
    for n, grown in enumerate((hx, cx, wx)):
        for side, (frm, at, to) in enumerate(((rows, 0, up), (STEPS, rows + STEPS, down))):
            halos.append(
                copy(
                    grown.at[pl.ds(frm, STEPS)],
                    grown.at[pl.ds(at, STEPS)],
                    halo_s.at[2 * n + side],
                    halo_r.at[2 * n + side],
                    "slab",
                    to,
                )
            )
    for item in halos:
        item.start()
    lax.fori_loop(EARLY, MIDDLE, every, 0)
    width = observed // slabs
    inverse_var = 1.0 / (os_ref[...] * os_ref[...])
    first_line = lax.broadcasted_iota(jnp.int32, (8, observed), 0) == 0
    observations = jnp.where(first_line, inverse_var, ov_ref[...])
    observations = pltpu.roll(observations, lax.rem(observed - width * slab, observed), 1)
    inside = lax.broadcasted_iota(jnp.int32, (8, LANES), 1) < width
    observations = jnp.where(inside, observations[:, 0:LANES], 0.0)

    for item in halos:
        item.wait_recv()
    head, perm, source = hx[...], cx[...], wx[...]
    open_first = jnp.where(slab == 0, 0.0, 1.0)
    open_last = jnp.where(slab == slabs - 1, 0.0, 1.0)
    for k in range(STEPS):
        head = advance(head, perm, source, open_first, open_last, k, rows)
        perm, source = perm[1:-1], source[1:-1]
    fore[...] = head
    w_ref[...] = jnp.zeros_like(w_ref)
    for i in range(rows):
        high, low = split(head[i])
        w_ref[0:local, cols * i : cols * i + cols] = high
        w_ref[16 : 16 + local, cols * i : cols * i + cols] = low

    def product(high_ref, low_ref, b):
        total = jnp.dot(w_ref[...], high_ref[b], preferred_element_type=F32)
        return total + jnp.dot(w_ref[...], low_ref[b], preferred_element_type=F32)

    shares = LANES // width
    each = local // shares
    line = lax.broadcasted_iota(jnp.int32, (32, 32), 0)
    col = lax.broadcasted_iota(jnp.int32, (32, 32), 1)
    wanted = (line // 8) * each + lax.rem(line, 8)
    valid = lax.rem(line, 8) < each
    gather = jnp.where(valid & ((col == wanted) | (col == wanted + 16)), 1.0, 0.0)
    lane = lax.broadcasted_iota(jnp.int32, (8, LANES), 1) // width
    for b in range(obs_blocks):
        total = mm(gather, product(ohi, olo, b))
        for half in range(BLOCK // LANES):
            block = total[:, LANES * half : LANES * half + LANES]
            for u in range(shares):
                chunk = None
                for g in range(shares):
                    piece = pltpu.roll(block[8 * g : 8 * g + 8], (width * (g - u)) % LANES, 1)
                    chunk = piece if g == 0 else jnp.where(lane == g, piece, chunk)
                po[(b * (BLOCK // LANES) + half) * shares + u] = chunk[0:4]
    send_obs.start()
    send_fore.start()
    ro[slab] = po[slab]

    def whole(b, carry):
        total = product(khi, klo, b)
        total = total[0:16] + total[16:32]
        for half in range(BLOCK // LANES):
            part[b * (BLOCK // LANES) + half] = total[0:local, LANES * half : LANES * half + LANES]
        return carry

    lax.fori_loop(0, FIRST, whole, 0)
    lax.fori_loop(MIDDLE, LATE, every, 0)
    send_obs.arrive()
    total = total_of(ro)
    mine[...] = total
    ao[member] = total
    send_mine.start()
    lax.fori_loop(LATE, blocks, every, 0)
    lax.fori_loop(FIRST, blocks, whole, 0)
    send_part.start()
    send_obs.drain()
    send_mine.arrive()
    lane = lax.broadcasted_iota(jnp.int32, (4, LANES), 1)
    for n in range(groups):
        tile = ao[n]
        for g in range(shares):
            piece = tile if g == 0 else pltpu.roll(tile, LANES - width * g, 1)
            at = local * n + each * g
            flat[at : at + each, :] = jnp.where(lane < width, piece, 0.0)[0:each]
    predicted = flat[...]
    centre = jnp.sum(predicted, axis=0, keepdims=True) * (1.0 / members)
    anomaly = predicted - centre
    weight = observations[0:1]
    gram = mm_nt(anomaly, anomaly * weight)
    rhs = mm_nt(jnp.broadcast_to(weight * (observations[1:2] - centre), (8, LANES)), anomaly)
    size = members // 3
    top = jnp.concatenate([gram[0:size, 0:size], gram[2 * size :, 2 * size :]], axis=1)
    pieces = [top, gram[size:, 0 : 2 * size], rhs[:, 0:LANES]]
    pieces.append(jnp.concatenate([rhs[:, LANES:], jnp.zeros((8, 2 * LANES - members), F32)], axis=1))
    height = gpart.shape[1]
    pieces.append(jnp.zeros((slabs * height - members - 16, LANES), F32))
    gpart[...] = jnp.concatenate(pieces, axis=0).reshape(slabs, height, LANES)
    send_gram.start()
    rs[slab] = part[slab]
    gred[slab] = gpart[slab]
    send_mine.drain()
    send_gram.arrive()
    gall[slab] = total_of(gred)
    send_sum.start()
    send_gram.drain()
    send_fore.arrive()
    pile[member] = fore[member]
    for n in range(groups):
        flat[local * n : local * n + local, :] = pile[n]
    spread = flat[...]
    centre = jnp.sum(spread, axis=0, keepdims=True) * (1.0 / members)
    spread = spread - centre
    send_part.arrive()
    total = jnp.concatenate([total_of(rs), jnp.zeros((LANES - local, LANES), F32)], axis=0)
    turned[...] = total.T.reshape(groups, own, LANES)
    send_sum.arrive()
    send_own.start()
    got[member] = turned[member]
    packed = gall[...].reshape(slabs * height, LANES)
    rhs = jnp.concatenate(
        [packed[members : members + 1], packed[members + 8 : members + 9]], axis=1
    )[:, 0:members]
    mix = transform(packed[0:members], rhs, members)
    flat[...] = centre + mm(mix, spread)
    for n in range(groups):
        snd[n] = flat[local * n : local * n + local, :]
    send_back.start()
    back[member] = snd[member]
    send_own.arrive()
    total = jnp.zeros((own, 2 * LANES), F32)
    for n in range(groups):
        tile = jnp.concatenate([got[n], jnp.zeros((own, LANES), F32)], axis=1)
        total += tile if n == 0 else pltpu.roll(tile, local * n, 1)
    own_ref[...] = total[:, 0:members]
    for item in halos:
        item.wait_send()
    send_fore.drain()
    send_part.drain()
    send_sum.drain()
    send_own.drain()
    send_back.arrive()
    for i in range(rows):
        ret_ref[:, i, :] = back[i]
    send_back.drain()


def shards(
    fluid_head_start,
    conductivity_matrix,
    well_rates,
    cell_layer,
    pixel_coords,
    obs_index,
    obs_value,
    obs_sigma,
):
    local, rows, cols = fluid_head_start.shape
    groups = lax.axis_size("member")
    slabs = lax.axis_size("slab")
    members = local * groups
    pixels = pixel_coords.shape[1]
    observed = obs_index.shape[0]
    own = pixels // (groups * slabs)
    height = 256 // slabs
    place = pl.BlockSpec(memory_space=pltpu.VMEM)
    tall = rows + 2 * STEPS

    def f32(*shape):
        return pltpu.VMEM(shape, F32)

    def bf16(*shape):
        return pltpu.VMEM(shape, BF16)

    def pair(shape):
        return [pltpu.SemaphoreType.DMA(shape)] * 2

    body = lambda *refs: cycle_kernel(rows * slabs, *refs)
    returned, own_part = pl.pallas_call(
        body,
        name="cycle",
        out_shape=(
            jax.ShapeDtypeStruct((local, rows, cols), F32),
            jax.ShapeDtypeStruct((own, members), F32),
        ),
        in_specs=[place] * 8,
        out_specs=(place, place),
        scratch_shapes=[
            f32(tall, local, cols),
            f32(tall, local, cols),
            f32(tall, 1, cols),
            f32(rows, local, cols),
            bf16(32, rows * cols),
            f32(rows, cols, LANES),
            f32(rows, cols, LANES),
            bf16(pixels // BLOCK, rows * cols, BLOCK),
            bf16(pixels // BLOCK, rows * cols, BLOCK),
            bf16(observed // BLOCK, rows * cols, BLOCK),
            bf16(observed // BLOCK, rows * cols, BLOCK),
            f32(2 * pixels // LANES, LANES),
            f32(8, observed),
            f32(2, pixels),
            f32(slabs, 4, LANES),
            f32(slabs, 4, LANES),
            f32(4, LANES),
            f32(groups, 4, LANES),
            f32(members, LANES),
            f32(slabs, local, LANES),
            f32(slabs, local, LANES),
            f32(groups, own, LANES),
            f32(groups, own, LANES),
            f32(slabs, height, LANES),
            f32(slabs, height, LANES),
            f32(slabs, height, LANES),
            f32(groups, local, cols),
            f32(groups, local, cols),
            f32(groups, local, cols),
            *pair((6,)),
            *(pair(()) * 8),
        ],
        compiler_params=pltpu.CompilerParams(
            collective_id=0, has_side_effects=True, vmem_limit_bytes=60 * 1024 * 1024
        ),
    )(
        fluid_head_start,
        conductivity_matrix,
        well_rates,
        cell_layer,
        pixel_coords,
        obs_index[None],
        obs_value[None],
        obs_sigma[None],
    )
    return (returned, own_part)


def solution(mesh):
    return jax.shard_map(
        shards,
        mesh=mesh,
        in_specs=(
            P("member", "slab", None),
            P("member", "slab", None),
            P("slab", None),
            P("slab", None),
            P(),
            P(),
            P(),
            P(),
        ),
        out_specs=(P("member", "slab", None), P(("member", "slab"), None)),
        check_vma=False,
    )
```

```python
import math

import jax
import jax.numpy as jnp
from jax import lax
from jax.experimental import pallas as pl
from jax.experimental.pallas import tpu as pltpu
from jax.sharding import PartitionSpec as P

STEPS = 4
time_step = 0.15
pixel_span = 64.0
top_depth = 2.0
F32 = jnp.float32
BF16 = jnp.bfloat16
HIGHEST = lax.Precision.HIGHEST
MESH = pl.DeviceIdType.MESH
BLOCK = 256
LANES = 128
EARLY = 3
MIDDLE = 9
LATE = 11
FIRST = 7
DEEP = 4


def split(value):
    high = value.astype(BF16)
    return high, (value - high.astype(F32)).astype(BF16)


def twice(value):
    return jnp.concatenate([value, value], axis=1)


def dot(a, b, dims):
    return lax.dot_general(a, b, (dims, ((), ())), precision=HIGHEST, preferred_element_type=F32)


def mm(a, b):
    return dot(a, b, ((1,), (0,)))


def mm_tn(a, b):
    return dot(a, b, ((0,), (0,)))


def mm_nt(a, b):
    return dot(a, b, ((1,), (1,)))


def inverse_factor(block):
    size = block.shape[0]
    wide = 2 * size
    count = size // 8
    sub = lax.broadcasted_iota(jnp.int32, (8, wide), 0)
    lane = lax.broadcasted_iota(jnp.int32, (8, wide), 1)

    def full(value):
        return jnp.broadcast_to(value, (8, wide))

    tiles = []
    for t in range(count):
        unit = jnp.where(lane == sub + (8 * t + size), 1.0, 0.0)
        tiles.append(jnp.concatenate([block[8 * t : 8 * t + 8], unit[:, size:]], axis=1))
    out = []
    for q in range(count):
        start = 8 * q
        cols = [
            [full(tiles[t][:, start + j : start + j + 1]) for t in range(q, count)] for j in range(8)
        ]
        lines = []
        top = tiles[q]
        pivots = None
        for k in range(0, 8, 2):
            left, right = cols[k], cols[k + 1]
            a = full(left[0][k : k + 1, :])
            b = full(left[0][k + 1 : k + 2, :])
            d = full(right[0][k + 1 : k + 2, :])
            det = a * d - b * b
            inv = 1.0 / det
            for j in range(k + 2, 8):
                u = full(left[0][j : j + 1, :])
                v = full(right[0][j : j + 1, :])
                p = (d * u - b * v) * inv
                r = (a * v - b * u) * inv
                cols[j] = [c - (x * p + y * r) for c, x, y in zip(cols[j], left, right)]
            u = full(top[k : k + 1, :])
            v = full(top[k + 1 : k + 2, :])
            p = (d * u - b * v) * inv
            r = (a * v - b * u) * inv
            lines += [p, r]
            ratio = 1.0 / a
            first = jnp.where(sub == k, a, det * ratio)
            pivots = first if k == 0 else jnp.where(sub >= k, first, pivots)
            step = left[0] * p + right[0] * r
            top = top - jnp.where(sub > k + 1, step, jnp.where(sub == k + 1, (b * ratio) * u, 0.0))
        out.append(top[:, size:] * lax.rsqrt(pivots)[:, size:])
        for t in range(q + 1, count):
            for k in range(8):
                tiles[t] = tiles[t] - cols[k][t - q] * lines[k]
    return jnp.concatenate(out, axis=0)


def transform(packed, rhs, members):
    size = members // 3
    row = lax.broadcasted_iota(jnp.int32, (members, 2 * size), 0)
    col = lax.broadcasted_iota(jnp.int32, (members, 2 * size), 1)
    gram = packed + jnp.where(row == col, members - 1.0, 0.0)
    corner = packed[0:size, size:] + jnp.where(row == col, members - 1.0, 0.0)[0:size, 0:size]
    l0 = inverse_factor(gram[0:size, 0:size])
    t0 = mm_nt(l0, gram[size:, 0:size])
    s1 = gram[size:, size:] - mm_tn(t0, t0[:, 0:size])
    z1 = -mm_tn(t0, l0)
    l1 = inverse_factor(s1[0:size])
    t1 = mm_nt(l1, s1[size:])
    l10 = mm(l1, z1[0:size])
    s2 = corner - mm_tn(t0[:, size:], t0[:, size:]) - mm_tn(t1, t1)
    z2 = jnp.concatenate([z1[size:] - mm_tn(t1, l10), -mm_tn(t1, l1)], axis=1)
    l2 = inverse_factor(s2)
    l20 = mm(l2, z2)
    zero = jnp.zeros((size, size), F32)
    inverse = jnp.concatenate(
        [
            jnp.concatenate([l0, zero, zero], axis=1),
            jnp.concatenate([l10, l1, zero], axis=1),
            jnp.concatenate([l20, l2], axis=1),
        ],
        axis=0,
    )
    reduced = jnp.sum(inverse * rhs, axis=1, keepdims=True)
    weights = jnp.sum(inverse * reduced, axis=0, keepdims=True)
    return weights + math.sqrt(members - 1.0) * inverse


def advance(head, perm, source, open_first, open_last, first_row, rows):
    mobility = perm * (1.0 + 0.5 * jnp.tanh(head))
    last = head.shape[0] - 1
    cols = head.shape[2]
    flux = 0.5 * (mobility[1:] + mobility[:-1]) * (head[1:] - head[:-1])
    parts = [flux[i : i + 1] for i in range(last)]
    near, far = STEPS - 1 - first_row, STEPS - 1 + rows - first_row
    parts[near] = parts[near] * open_first
    parts[far] = parts[far] * open_last
    flux = jnp.concatenate(parts, axis=0)
    inner = head[1:-1]
    own = mobility[1:-1]
    lane = lax.broadcasted_iota(jnp.int32, inner.shape, 2)
    along = 0.5 * (jnp.roll(own, -1, axis=2) + own) * (jnp.roll(inner, -1, axis=2) - inner)
    along = jnp.where(lane < cols - 1, along, 0.0)
    back = jnp.where(lane > 0, jnp.roll(along, 1, axis=2), 0.0)
    inflow = (flux[1:] - flux[:-1]) + (along - back)
    return inner + time_step * (inflow + source[1:-1])


def cycle_kernel(total_rows, *refs):
    arguments, staged, staged_s = refs[:8], refs[-9:-1], refs[-1]
    refs = refs[:-9]
    head_ref, cond_ref, well_ref, lay_ref, pc_ref, oi_ref, ov_ref, os_ref = staged
    ret_ref, own_ref = refs[8:10]
    hx, cx, wx, fore, w_ref, h2_ref, vh_ref, khi, klo, ohi, olo, place, where = refs[10:23]
    pcs, po, ro, mine, ao, flat, part, rs, turned, got, gpart, gred, gall, pile, snd, back = refs[23:39]
    halo_s, halo_r, out_s, out_r, ro_s, ro_r, ao_s, ao_r = refs[39:47]
    g1_s, g1_r, rs_s, rs_r, g2_s, g2_r, tu_s, tu_r, rt_s, rt_r = refs[47:]

    slab, member = lax.axis_index("slab"), lax.axis_index("member")
    slabs, groups = lax.axis_size("slab"), lax.axis_size("member")
    local, rows, cols = head_ref.shape
    members = local * groups
    pixels = pc_ref.shape[1]
    observed = oi_ref.shape[1]
    blocks, obs_blocks = pixels // BLOCK, observed // BLOCK
    row_pitch, col_pitch = pixel_span / total_rows, pixel_span / cols
    volume = pixel_span * pixel_span / (total_rows * cols)

    def other(i, axis):
        me, n = (slab, slabs) if axis == "slab" else (member, groups)
        return lax.rem(me + i, n)

    def peers(axis, body):
        n = slabs if axis == "slab" else groups

        def step(i, carry):
            body(other(i, axis))
            return carry

        lax.fori_loop(1, n, step, 0)

    def far_first(axis, body):
        inner = groups // DEEP if axis == "member" else slabs // DEEP
        for dz in (2, 1, 3, 0):

            def step(i, carry):
                if axis == "member":
                    to = lax.rem(member // DEEP + i, inner) * DEEP
                    to = to + lax.rem(member + dz, DEEP)
                else:
                    wide = 2 * DEEP
                    to = lax.rem(slab // wide + i // 2, slabs // wide) * wide
                    to = to + lax.rem(slab // 2 + dz, DEEP) * 2 + lax.rem(slab + i, 2)
                body(to)
                return carry

            lax.fori_loop(1 if dz == 0 else 0, inner, step, 0)

    def copy(src, dst, ssem, rsem, axis, to):
        return pltpu.make_async_remote_copy(
            src_ref=src,
            dst_ref=dst,
            send_sem=ssem,
            recv_sem=rsem,
            device_id={axis: to},
            device_id_type=MESH,
        )

    class Exchange:
        def __init__(self, axis, src, dst, ssem, rsem):
            self.axis, self.src, self.dst, self.ssem, self.rsem = axis, src, dst, ssem, rsem
            self.me = slab if axis == "slab" else member

        def one(self, to):
            copy(self.src(to), self.dst.at[self.me], self.ssem, self.rsem, self.axis, to).start()

        def start(self):
            far_first(self.axis, self.one)

        def every(self):
            part = self.dst.at[pl.ds(0, self.dst.shape[0] - 1)]
            return copy(part, part, self.ssem, self.rsem, self.axis, other(1, self.axis))

        def arrive(self):
            self.every().wait_recv()

        def drain(self):
            self.every().wait_send()

    def total_of(ref):
        value = ref[0]
        for n in range(1, ref.shape[0]):
            value += ref[n]
        return value

    send_fore = Exchange("member", lambda to: fore.at[to], pile, out_s, out_r)
    send_obs = Exchange("slab", lambda to: po.at[to], ro, ro_s, ro_r)
    send_mine = Exchange("member", lambda to: mine, ao, ao_s, ao_r)
    send_gram = Exchange("slab", lambda to: gpart.at[to], gred, g1_s, g1_r)
    send_part = Exchange("slab", lambda to: part.at[to], rs, rs_s, rs_r)
    send_sum = Exchange("slab", lambda to: gall.at[slab], gall, g2_s, g2_r)
    send_own = Exchange("member", lambda to: turned.at[to], got, tu_s, tu_r)
    send_back = Exchange("member", lambda to: snd.at[to], back, rt_s, rt_r)

    loads = [
        pltpu.make_async_copy(src, dst, staged_s.at[n])
        for n, (src, dst) in enumerate(zip(arguments, staged))
    ]
    for item in loads:
        item.start()
    barrier = pltpu.get_barrier_semaphore()
    for axis in ("slab", "member"):
        peers(
            axis,
            lambda to: pl.semaphore_signal(barrier, inc=1, device_id={axis: to}, device_id_type=MESH),
        )

    for item in loads:
        item.wait()
    for i in range(rows):
        hx[STEPS + i] = head_ref[:, i, :]
        cx[STEPS + i] = cond_ref[:, i, :]
        wx[STEPS + i] = well_ref[i : i + 1, :]
    depth = top_depth + lay_ref[...].astype(F32)
    depth = jnp.concatenate([depth, jnp.zeros((cols - rows, cols), F32)], axis=0).T
    for i in range(rows):
        column = depth[:, i : i + 1]
        h2_ref[i] = jnp.broadcast_to(column * column, (cols, LANES))
        vh_ref[i] = jnp.broadcast_to(volume * column, (cols, LANES))
    cell_y = (lax.broadcasted_iota(jnp.int32, (cols, BLOCK), 0).astype(F32) + 0.5) * col_pitch
    first = (slab * rows).astype(F32)

    def evaluate(coords_ref, high_ref, low_ref):
        def step(n, carry):
            b = lax.rem(n + slab // 2, coords_ref.shape[1] // BLOCK)
            at = pl.multiple_of(b * BLOCK, BLOCK)
            coords = coords_ref[0:2, pl.ds(at, BLOCK)].astype(F32)
            delta_y = cell_y - coords[1:2]
            dy2 = delta_y * delta_y
            for i in range(rows):
                delta_x = (first + (i + 0.5)) * row_pitch - coords[0:1]
                radius = (dy2 + delta_x * delta_x) + twice(h2_ref[i])
                inv = lax.rsqrt(radius)
                high, low = split(twice(vh_ref[i]) * (inv * inv * inv))
                high_ref[b, cols * i : cols * i + cols, :] = high
                low_ref[b, cols * i : cols * i + cols, :] = low
            return carry

        return step

    groups_of = pixels // LANES
    for c in range(2):
        for n in range(groups_of):
            place[groups_of * c + n : groups_of * c + n + 1, :] = pc_ref[
                c : c + 1, LANES * n : LANES * n + LANES
            ].astype(F32)
    own = LANES // groups
    near = slabs * own // LANES
    line = lax.broadcasted_iota(jnp.int32, (groups, LANES), 0)
    lane = lax.broadcasted_iota(jnp.int32, (groups, LANES), 1)
    widen = jnp.where(lane // own == line, 1.0, 0.0).astype(BF16)
    line = lax.broadcasted_iota(jnp.int32, (LANES, LANES), 0)
    lane = lax.broadcasted_iota(jnp.int32, (LANES, LANES), 1)
    same = lax.rem(line, own) == lax.rem(lane, own)
    for c in range(2):
        for h in range(near):
            table = place[pl.ds(groups_of * c + h, groups, stride=near), :].astype(BF16)
            wide = lax.dot_general(
                table, widen, (((0,), (0,)), ((), ())), preferred_element_type=F32
            )
            wide = jnp.sum(jnp.where(same, wide, 0.0).reshape(LANES // own, own, LANES), axis=1)
            for n in range(LANES // own):
                at = (h * (LANES // own) + n) * LANES
                pcs[c : c + 1, at : at + LANES] = wide[n : n + 1]
    high_part, low_part = oi_ref[...] // LANES, lax.rem(oi_ref[...], LANES)
    line = lax.broadcasted_iota(jnp.int32, (groups_of, observed), 0)
    pick = jnp.where(line == high_part, 1.0, 0.0).astype(BF16)
    spot = lax.broadcasted_iota(jnp.int32, (LANES, observed), 0) == low_part
    for c in range(2):
        table = place[groups_of * c : groups_of * c + groups_of, :].astype(BF16)
        found = lax.dot_general(table, pick, (((0,), (0,)), ((), ())), preferred_element_type=F32)
        where[c : c + 1, :] = jnp.sum(jnp.where(spot, found, 0.0), axis=0, keepdims=True)
    lax.fori_loop(0, obs_blocks, evaluate(where, ohi, olo), 0)
    every = evaluate(pcs, khi, klo)
    lax.fori_loop(0, EARLY, every, 0)

    pl.semaphore_wait(barrier, slabs - 1 + groups - 1)

    up, down = other(1, "slab"), other(slabs - 1, "slab")
    halos = []
    for n, grown in enumerate((hx, cx, wx)):
        for side, (frm, at, to) in enumerate(((rows, 0, up), (STEPS, rows + STEPS, down))):
            halos.append(
                copy(
                    grown.at[pl.ds(frm, STEPS)],
                    grown.at[pl.ds(at, STEPS)],
                    halo_s.at[2 * n + side],
                    halo_r.at[2 * n + side],
                    "slab",
                    to,
                )
            )
    for item in halos:
        item.start()
    lax.fori_loop(EARLY, MIDDLE, every, 0)
    width = observed // slabs
    inverse_var = 1.0 / (os_ref[...] * os_ref[...])
    first_line = lax.broadcasted_iota(jnp.int32, (8, observed), 0) == 0
    observations = jnp.where(first_line, inverse_var, ov_ref[...])
    observations = pltpu.roll(observations, lax.rem(observed - width * slab, observed), 1)
    inside = lax.broadcasted_iota(jnp.int32, (8, LANES), 1) < width
    observations = jnp.where(inside, observations[:, 0:LANES], 0.0)

    for item in halos:
        item.wait_recv()
    head, perm, source = hx[...], cx[...], wx[...]
    open_first = jnp.where(slab == 0, 0.0, 1.0)
    open_last = jnp.where(slab == slabs - 1, 0.0, 1.0)
    for k in range(STEPS):
        head = advance(head, perm, source, open_first, open_last, k, rows)
        perm, source = perm[1:-1], source[1:-1]
    fore[...] = head
    w_ref[...] = jnp.zeros_like(w_ref)
    for i in range(rows):
        high, low = split(head[i])
        w_ref[0:local, cols * i : cols * i + cols] = high
        w_ref[16 : 16 + local, cols * i : cols * i + cols] = low

    def product(high_ref, low_ref, b):
        total = jnp.dot(w_ref[...], high_ref[b], preferred_element_type=F32)
        return total + jnp.dot(w_ref[...], low_ref[b], preferred_element_type=F32)

    shares = LANES // width
    each = local // shares
    line = lax.broadcasted_iota(jnp.int32, (32, 32), 0)
    col = lax.broadcasted_iota(jnp.int32, (32, 32), 1)
    wanted = (line // 8) * each + lax.rem(line, 8)
    valid = lax.rem(line, 8) < each
    gather = jnp.where(valid & ((col == wanted) | (col == wanted + 16)), 1.0, 0.0)
    lane = lax.broadcasted_iota(jnp.int32, (8, LANES), 1) // width
    for n in range(obs_blocks):
        b = lax.rem(n + slab // (slabs // obs_blocks), obs_blocks)
        total = mm(gather, product(ohi, olo, b))
        for half in range(BLOCK // LANES):
            block = total[:, LANES * half : LANES * half + LANES]
            for u in range(shares):
                chunk = None
                for g in range(shares):
                    piece = pltpu.roll(block[8 * g : 8 * g + 8], (width * (g - u)) % LANES, 1)
                    chunk = piece if g == 0 else jnp.where(lane == g, piece, chunk)
                po[(b * (BLOCK // LANES) + half) * shares + u] = chunk[0:4]
        count = slabs // obs_blocks

        def send(i, carry):
            to = b * count + lax.rem(i + slab, count)

            @pl.when(to != slab)
            def _():
                send_obs.one(to)

            return carry

        lax.fori_loop(0, count, send, 0)
    send_fore.start()
    ro[slab] = po[slab]

    def whole(n, carry):
        b = lax.rem(n + slab // 2, blocks)
        total = product(khi, klo, b)
        total = total[0:16] + total[16:32]
        for half in range(BLOCK // LANES):
            part[b * (BLOCK // LANES) + half] = total[0:local, LANES * half : LANES * half + LANES]
        return carry

    def send_parts(n, carry):
        to = lax.rem(n + (slab // 2) * (BLOCK // LANES), slabs)

        @pl.when(to != slab)
        def _():
            send_part.one(to)

        return carry

    burst = FIRST * (BLOCK // LANES)
    lax.fori_loop(0, FIRST, whole, 0)
    lax.fori_loop(0, burst, send_parts, 0)
    lax.fori_loop(MIDDLE, LATE, every, 0)
    send_obs.arrive()
    total = total_of(ro)
    mine[...] = total
    ao[member] = total
    send_mine.start()
    lax.fori_loop(LATE, blocks, every, 0)
    lax.fori_loop(FIRST, blocks, whole, 0)
    lax.fori_loop(burst, slabs, send_parts, 0)
    send_obs.drain()
    send_mine.arrive()
    lane = lax.broadcasted_iota(jnp.int32, (4, LANES), 1)
    for n in range(groups):
        tile = ao[n]
        for g in range(shares):
            piece = tile if g == 0 else pltpu.roll(tile, LANES - width * g, 1)
            at = local * n + each * g
            flat[at : at + each, :] = jnp.where(lane < width, piece, 0.0)[0:each]
    predicted = flat[...]
    centre = jnp.sum(predicted, axis=0, keepdims=True) * (1.0 / members)
    anomaly = predicted - centre
    weight = observations[0:1]
    gram = mm_nt(anomaly, anomaly * weight)
    rhs = mm_nt(jnp.broadcast_to(weight * (observations[1:2] - centre), (8, LANES)), anomaly)
    size = members // 3
    top = jnp.concatenate([gram[0:size, 0:size], gram[2 * size :, 2 * size :]], axis=1)
    pieces = [top, gram[size:, 0 : 2 * size], rhs[:, 0:LANES]]
    pieces.append(jnp.concatenate([rhs[:, LANES:], jnp.zeros((8, 2 * LANES - members), F32)], axis=1))
    height = gpart.shape[1]
    pieces.append(jnp.zeros((slabs * height - members - 16, LANES), F32))
    gpart[...] = jnp.concatenate(pieces, axis=0).reshape(slabs, height, LANES)
    send_gram.start()
    rs[slab] = part[slab]
    gred[slab] = gpart[slab]
    send_mine.drain()
    send_gram.arrive()
    gall[slab] = total_of(gred)
    send_sum.start()
    send_gram.drain()
    send_fore.arrive()
    pile[member] = fore[member]
    for n in range(groups):
        flat[local * n : local * n + local, :] = pile[n]
    spread = flat[...]
    centre = jnp.sum(spread, axis=0, keepdims=True) * (1.0 / members)
    spread = spread - centre
    send_part.arrive()
    total = jnp.concatenate([total_of(rs), jnp.zeros((LANES - local, LANES), F32)], axis=0)
    turned[...] = total.T.reshape(groups, own, LANES)
    send_sum.arrive()
    send_own.start()
    got[member] = turned[member]
    packed = gall[...].reshape(slabs * height, LANES)
    rhs = jnp.concatenate(
        [packed[members : members + 1], packed[members + 8 : members + 9]], axis=1
    )[:, 0:members]
    mix = transform(packed[0:members], rhs, members)
    flat[...] = centre + mm(mix, spread)
    for n in range(groups):
        snd[n] = flat[local * n : local * n + local, :]
    send_back.start()
    back[member] = snd[member]
    send_own.arrive()
    total = jnp.zeros((own, 2 * LANES), F32)
    for n in range(groups):
        tile = jnp.concatenate([got[n], jnp.zeros((own, LANES), F32)], axis=1)
        total += tile if n == 0 else pltpu.roll(tile, local * n, 1)
    own_ref[...] = total[:, 0:members]
    for item in halos:
        item.wait_send()
    send_fore.drain()
    send_part.drain()
    send_sum.drain()
    send_own.drain()
    send_back.arrive()
    for i in range(rows):
        ret_ref[:, i, :] = back[i]
    send_back.drain()


def shards(
    fluid_head_start,
    conductivity_matrix,
    well_rates,
    cell_layer,
    pixel_coords,
    obs_index,
    obs_value,
    obs_sigma,
):
    local, rows, cols = fluid_head_start.shape
    groups = lax.axis_size("member")
    slabs = lax.axis_size("slab")
    members = local * groups
    pixels = pixel_coords.shape[1]
    observed = obs_index.shape[0]
    own = pixels // (groups * slabs)
    height = 256 // slabs
    place = pl.BlockSpec(memory_space=pltpu.VMEM)
    tall = rows + 2 * STEPS

    def f32(*shape):
        return pltpu.VMEM(shape, F32)

    def bf16(*shape):
        return pltpu.VMEM(shape, BF16)

    def pair(shape):
        return [pltpu.SemaphoreType.DMA(shape)] * 2

    body = lambda *refs: cycle_kernel(rows * slabs, *refs)
    arguments = (
        fluid_head_start,
        conductivity_matrix,
        well_rates,
        cell_layer,
        pixel_coords,
        obs_index[None],
        obs_value[None],
        obs_sigma[None],
    )
    returned, own_part = pl.pallas_call(
        body,
        name="cycle",
        out_shape=(
            jax.ShapeDtypeStruct((local, rows, cols), F32),
            jax.ShapeDtypeStruct((own, members), F32),
        ),
        in_specs=[pl.BlockSpec(memory_space=pltpu.HBM)] * 8,
        out_specs=(place, place),
        scratch_shapes=[
            f32(tall, local, cols),
            f32(tall, local, cols),
            f32(tall, 1, cols),
            f32(rows, local, cols),
            bf16(32, rows * cols),
            f32(rows, cols, LANES),
            f32(rows, cols, LANES),
            bf16(pixels // BLOCK, rows * cols, BLOCK),
            bf16(pixels // BLOCK, rows * cols, BLOCK),
            bf16(observed // BLOCK, rows * cols, BLOCK),
            bf16(observed // BLOCK, rows * cols, BLOCK),
            f32(2 * pixels // LANES, LANES),
            f32(8, observed),
            f32(2, pixels),
            f32(slabs, 4, LANES),
            f32(slabs, 4, LANES),
            f32(4, LANES),
            f32(groups, 4, LANES),
            f32(members, LANES),
            f32(slabs, local, LANES),
            f32(slabs, local, LANES),
            f32(groups, own, LANES),
            f32(groups, own, LANES),
            f32(slabs, height, LANES),
            f32(slabs, height, LANES),
            f32(slabs, height, LANES),
            f32(groups, local, cols),
            f32(groups, local, cols),
            f32(groups, local, cols),
            *pair((6,)),
            *(pair(()) * 8),
            *(pltpu.VMEM(value.shape, value.dtype) for value in arguments),
            pltpu.SemaphoreType.DMA((len(arguments),)),
        ],
        compiler_params=pltpu.CompilerParams(
            collective_id=0, has_side_effects=True, vmem_limit_bytes=52 * 1024 * 1024
        ),
    )(*(pltpu.with_memory_space_constraint(value, pltpu.HBM) for value in arguments))
    return (returned, own_part)


def solution(mesh):
    return jax.shard_map(
        shards,
        mesh=mesh,
        in_specs=(
            P("member", "slab", None),
            P("member", "slab", None),
            P("slab", None),
            P("slab", None),
            P(),
            P(),
            P(),
            P(),
        ),
        out_specs=(P("member", "slab", None), P(("member", "slab"), None)),
        check_vma=False,
    )
```

```python
import math

import jax
import jax.numpy as jnp
from jax import lax
from jax.experimental import pallas as pl
from jax.experimental.pallas import tpu as pltpu
from jax.sharding import PartitionSpec as P

STEPS = 4
time_step = 0.15
pixel_span = 64.0
top_depth = 2.0
F32 = jnp.float32
BF16 = jnp.bfloat16
HIGHEST = lax.Precision.HIGHEST
MESH = pl.DeviceIdType.MESH
BLOCK = 256
LANES = 128
EARLY = 3
MIDDLE = 9
LATE = 11
FIRST = 7
DEEP = 4


def split(value):
    high = value.astype(BF16)
    return high, (value - high.astype(F32)).astype(BF16)


def twice(value):
    return jnp.concatenate([value, value], axis=1)


def dot(a, b, dims):
    return lax.dot_general(a, b, (dims, ((), ())), precision=HIGHEST, preferred_element_type=F32)


def mm(a, b):
    return dot(a, b, ((1,), (0,)))


def mm_tn(a, b):
    return dot(a, b, ((0,), (0,)))


def mm_nt(a, b):
    return dot(a, b, ((1,), (1,)))


def inverse_factor(block):
    size = block.shape[0]
    wide = 2 * size
    count = size // 8
    sub = lax.broadcasted_iota(jnp.int32, (8, wide), 0)
    lane = lax.broadcasted_iota(jnp.int32, (8, wide), 1)

    def full(value):
        return jnp.broadcast_to(value, (8, wide))

    tiles = []
    for t in range(count):
        unit = jnp.where(lane == sub + (8 * t + size), 1.0, 0.0)
        tiles.append(jnp.concatenate([block[8 * t : 8 * t + 8], unit[:, size:]], axis=1))
    out = []
    for q in range(count):
        start = 8 * q
        cols = [
            [full(tiles[t][:, start + j : start + j + 1]) for t in range(q, count)] for j in range(8)
        ]
        lines = []
        top = tiles[q]
        pivots = None
        for k in range(0, 8, 2):
            left, right = cols[k], cols[k + 1]
            a = full(left[0][k : k + 1, :])
            b = full(left[0][k + 1 : k + 2, :])
            d = full(right[0][k + 1 : k + 2, :])
            det = a * d - b * b
            inv = 1.0 / det
            for j in range(k + 2, 8):
                u = full(left[0][j : j + 1, :])
                v = full(right[0][j : j + 1, :])
                p = (d * u - b * v) * inv
                r = (a * v - b * u) * inv
                cols[j] = [c - (x * p + y * r) for c, x, y in zip(cols[j], left, right)]
            u = full(top[k : k + 1, :])
            v = full(top[k + 1 : k + 2, :])
            p = (d * u - b * v) * inv
            r = (a * v - b * u) * inv
            lines += [p, r]
            ratio = 1.0 / a
            first = jnp.where(sub == k, a, det * ratio)
            pivots = first if k == 0 else jnp.where(sub >= k, first, pivots)
            step = left[0] * p + right[0] * r
            top = top - jnp.where(sub > k + 1, step, jnp.where(sub == k + 1, (b * ratio) * u, 0.0))
        out.append(top[:, size:] * lax.rsqrt(pivots)[:, size:])
        for t in range(q + 1, count):
            for k in range(8):
                tiles[t] = tiles[t] - cols[k][t - q] * lines[k]
    return jnp.concatenate(out, axis=0)


def transform(packed, rhs, members):
    size = members // 3
    row = lax.broadcasted_iota(jnp.int32, (members, 2 * size), 0)
    col = lax.broadcasted_iota(jnp.int32, (members, 2 * size), 1)
    gram = packed + jnp.where(row == col, members - 1.0, 0.0)
    corner = packed[0:size, size:] + jnp.where(row == col, members - 1.0, 0.0)[0:size, 0:size]
    l0 = inverse_factor(gram[0:size, 0:size])
    t0 = mm_nt(l0, gram[size:, 0:size])
    s1 = gram[size:, size:] - mm_tn(t0, t0[:, 0:size])
    z1 = -mm_tn(t0, l0)
    l1 = inverse_factor(s1[0:size])
    t1 = mm_nt(l1, s1[size:])
    l10 = mm(l1, z1[0:size])
    s2 = corner - mm_tn(t0[:, size:], t0[:, size:]) - mm_tn(t1, t1)
    z2 = jnp.concatenate([z1[size:] - mm_tn(t1, l10), -mm_tn(t1, l1)], axis=1)
    l2 = inverse_factor(s2)
    l20 = mm(l2, z2)
    zero = jnp.zeros((size, size), F32)
    inverse = jnp.concatenate(
        [
            jnp.concatenate([l0, zero, zero], axis=1),
            jnp.concatenate([l10, l1, zero], axis=1),
            jnp.concatenate([l20, l2], axis=1),
        ],
        axis=0,
    )
    reduced = jnp.sum(inverse * rhs, axis=1, keepdims=True)
    weights = jnp.sum(inverse * reduced, axis=0, keepdims=True)
    return weights + math.sqrt(members - 1.0) * inverse


def advance(head, perm, source, open_first, open_last, first_row, rows):
    mobility = perm * (1.0 + 0.5 * jnp.tanh(head))
    last = head.shape[0] - 1
    cols = head.shape[2]
    flux = 0.5 * (mobility[1:] + mobility[:-1]) * (head[1:] - head[:-1])
    parts = [flux[i : i + 1] for i in range(last)]
    near, far = STEPS - 1 - first_row, STEPS - 1 + rows - first_row
    parts[near] = parts[near] * open_first
    parts[far] = parts[far] * open_last
    flux = jnp.concatenate(parts, axis=0)
    inner = head[1:-1]
    own = mobility[1:-1]
    lane = lax.broadcasted_iota(jnp.int32, inner.shape, 2)
    along = 0.5 * (jnp.roll(own, -1, axis=2) + own) * (jnp.roll(inner, -1, axis=2) - inner)
    along = jnp.where(lane < cols - 1, along, 0.0)
    back = jnp.where(lane > 0, jnp.roll(along, 1, axis=2), 0.0)
    inflow = (flux[1:] - flux[:-1]) + (along - back)
    return inner + time_step * (inflow + source[1:-1])


def cycle_kernel(total_rows, *refs):
    arguments, staged, staged_s = refs[:8], refs[-9:-1], refs[-1]
    refs = refs[:-9]
    head_ref, cond_ref, well_ref, lay_ref, pc_ref, oi_ref, ov_ref, os_ref = staged
    ret_ref, own_ref = refs[8:10]
    hx, cx, wx, fore, w_ref, h2_ref, vh_ref, khi, klo, ohi, olo, place, where = refs[10:23]
    pcs, wo_ref, po, ro, mine, ao, flat, part, rs, turned, got, gpart, gred, gall, pile, snd, back = refs[23:40]
    halo_s, halo_r, out_s, out_r, ro_s, ro_r, ao_s, ao_r = refs[40:48]
    g1_s, g1_r, rs_s, rs_r, g2_s, g2_r, tu_s, tu_r, rt_s, rt_r = refs[48:]

    slab, member = lax.axis_index("slab"), lax.axis_index("member")
    slabs, groups = lax.axis_size("slab"), lax.axis_size("member")
    local, rows, cols = head_ref.shape
    members = local * groups
    pixels = pc_ref.shape[1]
    observed = oi_ref.shape[1]
    blocks, obs_blocks = pixels // BLOCK, observed // BLOCK
    row_pitch, col_pitch = pixel_span / total_rows, pixel_span / cols
    volume = pixel_span * pixel_span / (total_rows * cols)

    def other(i, axis):
        me, n = (slab, slabs) if axis == "slab" else (member, groups)
        return lax.rem(me + i, n)

    def peers(axis, body):
        n = slabs if axis == "slab" else groups

        def step(i, carry):
            body(other(i, axis))
            return carry

        lax.fori_loop(1, n, step, 0)

    def far_first(axis, body):
        if axis == "member":
            inner = groups // DEEP
            across = [lax.rem(member // DEEP + i, inner) * DEEP for i in range(inner)]
            along = [lax.rem(member + i, DEEP) for i in range(DEEP)]
            cores = [0]
        else:
            inner = slabs // (2 * DEEP)
            across = [lax.rem(slab // (2 * DEEP) + i, inner) * (2 * DEEP) for i in range(inner)]
            along = [lax.rem(slab // 2 + i, DEEP) * 2 for i in range(DEEP)]
            cores = [lax.rem(slab, 2), lax.rem(slab + 1, 2)]
        for dz in (2, 1, 3, 0):
            for i in range(inner):
                for c, core in enumerate(cores):
                    if dz or i or c:
                        body(across[i] + along[dz] + core)

    def copy(src, dst, ssem, rsem, axis, to):
        return pltpu.make_async_remote_copy(
            src_ref=src,
            dst_ref=dst,
            send_sem=ssem,
            recv_sem=rsem,
            device_id={axis: to},
            device_id_type=MESH,
        )

    class Exchange:
        def __init__(self, axis, src, dst, ssem, rsem):
            self.axis, self.src, self.dst, self.ssem, self.rsem = axis, src, dst, ssem, rsem
            self.me = slab if axis == "slab" else member

        def one(self, to):
            copy(self.src(to), self.dst.at[self.me], self.ssem, self.rsem, self.axis, to).start()

        def start(self):
            far_first(self.axis, self.one)

        def every(self, n=None):
            part = self.dst.at[pl.ds(0, n or self.dst.shape[0] - 1)]
            return copy(part, part, self.ssem, self.rsem, self.axis, other(1, self.axis))

        def arrive(self):
            self.every().wait_recv()

        def drain(self):
            self.every().wait_send()

    height = gpart.shape[1]
    owners = (members + 16 + height - 1) // height

    def total_of(ref):
        value = ref[0]
        for n in range(1, ref.shape[0]):
            value += ref[n]
        return value

    send_fore = Exchange("member", lambda to: fore.at[to], pile, out_s, out_r)
    send_obs = Exchange("slab", lambda to: po.at[to], ro, ro_s, ro_r)
    send_mine = Exchange("member", lambda to: mine, ao, ao_s, ao_r)
    send_gram = Exchange("slab", lambda to: gpart.at[to], gred, g1_s, g1_r)
    send_part = Exchange("slab", lambda to: part.at[to], rs, rs_s, rs_r)
    send_sum = Exchange("slab", lambda to: gall.at[slab], gall, g2_s, g2_r)
    send_own = Exchange("member", lambda to: turned.at[to], got, tu_s, tu_r)
    send_back = Exchange("member", lambda to: snd.at[to], back, rt_s, rt_r)

    loads = [
        pltpu.make_async_copy(src, dst, staged_s.at[n])
        for n, (src, dst) in enumerate(zip(arguments, staged))
    ]
    for item in loads:
        item.start()
    barrier = pltpu.get_barrier_semaphore()
    for axis in ("slab", "member"):
        peers(
            axis,
            lambda to: pl.semaphore_signal(barrier, inc=1, device_id={axis: to}, device_id_type=MESH),
        )

    for item in loads:
        item.wait()
    for i in range(rows):
        hx[STEPS + i] = head_ref[:, i, :]
        cx[STEPS + i] = cond_ref[:, i, :]
        wx[STEPS + i] = well_ref[i : i + 1, :]
    depth = top_depth + lay_ref[...].astype(F32)
    depth = jnp.concatenate([depth, jnp.zeros((cols - rows, cols), F32)], axis=0).T
    for i in range(rows):
        column = depth[:, i : i + 1]
        h2_ref[i] = jnp.broadcast_to(column * column, (cols, LANES))
        vh_ref[i] = jnp.broadcast_to(volume * column, (cols, LANES))
    cell_y = (lax.broadcasted_iota(jnp.int32, (cols, BLOCK), 0).astype(F32) + 0.5) * col_pitch
    first = (slab * rows).astype(F32)

    def evaluate(coords_ref, high_ref, low_ref):
        def step(n, carry):
            b = lax.rem(n + slab // 2, coords_ref.shape[1] // BLOCK)
            at = pl.multiple_of(b * BLOCK, BLOCK)
            coords = coords_ref[0:2, pl.ds(at, BLOCK)].astype(F32)
            delta_y = cell_y - coords[1:2]
            dy2 = delta_y * delta_y
            for i in range(rows):
                delta_x = (first + (i + 0.5)) * row_pitch - coords[0:1]
                radius = (dy2 + delta_x * delta_x) + twice(h2_ref[i])
                inv = lax.rsqrt(radius)
                high, low = split(twice(vh_ref[i]) * (inv * inv * inv))
                high_ref[b, cols * i : cols * i + cols, :] = high
                low_ref[b, cols * i : cols * i + cols, :] = low
            return carry

        return step

    groups_of = pixels // LANES
    for c in range(2):
        for n in range(groups_of):
            place[groups_of * c + n : groups_of * c + n + 1, :] = pc_ref[
                c : c + 1, LANES * n : LANES * n + LANES
            ].astype(F32)
    own = LANES // groups
    near = slabs * own // LANES
    line = lax.broadcasted_iota(jnp.int32, (groups, LANES), 0)
    lane = lax.broadcasted_iota(jnp.int32, (groups, LANES), 1)
    widen = jnp.where(lane // own == line, 1.0, 0.0).astype(BF16)
    line = lax.broadcasted_iota(jnp.int32, (LANES, LANES), 0)
    lane = lax.broadcasted_iota(jnp.int32, (LANES, LANES), 1)
    same = lax.rem(line, own) == lax.rem(lane, own)
    for c in range(2):
        for h in range(near):
            table = place[pl.ds(groups_of * c + h, groups, stride=near), :].astype(BF16)
            wide = lax.dot_general(
                table, widen, (((0,), (0,)), ((), ())), preferred_element_type=F32
            )
            wide = jnp.sum(jnp.where(same, wide, 0.0).reshape(LANES // own, own, LANES), axis=1)
            for n in range(LANES // own):
                at = (h * (LANES // own) + n) * LANES
                pcs[c : c + 1, at : at + LANES] = wide[n : n + 1]
    high_part, low_part = oi_ref[...] // LANES, lax.rem(oi_ref[...], LANES)
    line = lax.broadcasted_iota(jnp.int32, (groups_of, observed), 0)
    pick = jnp.where(line == high_part, 1.0, 0.0).astype(BF16)
    spot = lax.broadcasted_iota(jnp.int32, (LANES, observed), 0) == low_part
    for c in range(2):
        table = place[groups_of * c : groups_of * c + groups_of, :].astype(BF16)
        found = lax.dot_general(table, pick, (((0,), (0,)), ((), ())), preferred_element_type=F32)
        where[c : c + 1, :] = jnp.sum(jnp.where(spot, found, 0.0), axis=0, keepdims=True)
    lax.fori_loop(0, obs_blocks, evaluate(where, ohi, olo), 0)
    every = evaluate(pcs, khi, klo)
    lax.fori_loop(0, EARLY, every, 0)

    pl.semaphore_wait(barrier, slabs - 1 + groups - 1)

    up, down = other(1, "slab"), other(slabs - 1, "slab")
    halos = []
    for n, grown in enumerate((hx, cx, wx)):
        for side, (frm, at, to) in enumerate(((rows, 0, up), (STEPS, rows + STEPS, down))):
            halos.append(
                copy(
                    grown.at[pl.ds(frm, STEPS)],
                    grown.at[pl.ds(at, STEPS)],
                    halo_s.at[2 * n + side],
                    halo_r.at[2 * n + side],
                    "slab",
                    to,
                )
            )
    for item in halos:
        item.start()
    lax.fori_loop(EARLY, MIDDLE, every, 0)
    width = observed // slabs
    inverse_var = 1.0 / (os_ref[...] * os_ref[...])
    first_line = lax.broadcasted_iota(jnp.int32, (8, observed), 0) == 0
    observations = jnp.where(first_line, inverse_var, ov_ref[...])
    observations = pltpu.roll(observations, lax.rem(observed - width * slab, observed), 1)
    inside = lax.broadcasted_iota(jnp.int32, (8, LANES), 1) < width
    observations = jnp.where(inside, observations[:, 0:LANES], 0.0)

    for item in halos:
        item.wait_recv()
    head, perm, source = hx[...], cx[...], wx[...]
    open_first = jnp.where(slab == 0, 0.0, 1.0)
    open_last = jnp.where(slab == slabs - 1, 0.0, 1.0)
    for k in range(STEPS):
        head = advance(head, perm, source, open_first, open_last, k, rows)
        perm, source = perm[1:-1], source[1:-1]
    fore[...] = head
    w_ref[...] = jnp.zeros_like(w_ref)
    for i in range(rows):
        high, low = split(head[i])
        w_ref[0:local, cols * i : cols * i + cols] = high
        w_ref[16 : 16 + local, cols * i : cols * i + cols] = low

    shares = LANES // width
    each = local // shares
    line = lax.broadcasted_iota(jnp.int32, (64, 32), 0)
    col = lax.broadcasted_iota(jnp.int32, (64, 32), 1)
    wanted = lax.rem(line // 8, 4) * each + lax.rem(line, 8) + (line // 32) * 16
    valid = lax.rem(line, 8) < each
    gather = jnp.where(valid & (col == wanted), 1.0, 0.0).astype(BF16)
    wo_ref[...] = jnp.dot(gather, w_ref[...], preferred_element_type=F32).astype(BF16)
    lane = lax.broadcasted_iota(jnp.int32, (8, LANES), 1) // width
    for n in range(obs_blocks):
        b = lax.rem(n + slab // (slabs // obs_blocks), obs_blocks)
        total = jnp.dot(wo_ref[...], ohi[b], preferred_element_type=F32)
        total += jnp.dot(wo_ref[...], olo[b], preferred_element_type=F32)
        total = total[0:32] + total[32:64]
        for half in range(BLOCK // LANES):
            block = total[:, LANES * half : LANES * half + LANES]
            for u in range(shares):
                chunk = None
                for g in range(shares):
                    piece = pltpu.roll(block[8 * g : 8 * g + 8], (width * (g - u)) % LANES, 1)
                    chunk = piece if g == 0 else jnp.where(lane == g, piece, chunk)
                po[(b * (BLOCK // LANES) + half) * shares + u] = chunk[0:4]
        count = slabs // obs_blocks

        def send(i, carry):
            to = b * count + lax.rem(i + slab, count)

            @pl.when(to != slab)
            def _():
                send_obs.one(to)

            return carry

        lax.fori_loop(0, count, send, 0)
    send_fore.start()
    ro[slab] = po[slab]

    def whole(n, carry):
        b = lax.rem(n + slab // 2, blocks)
        total = jnp.dot(w_ref[...], khi[b], preferred_element_type=F32)
        total += jnp.dot(w_ref[...], klo[b], preferred_element_type=F32)
        total = total[0:16] + total[16:32]
        for half in range(BLOCK // LANES):
            part[b * (BLOCK // LANES) + half] = total[0:local, LANES * half : LANES * half + LANES]
        return carry

    def send_parts(n, carry):
        to = lax.rem(n + (slab // 2) * (BLOCK // LANES), slabs)

        @pl.when(to != slab)
        def _():
            send_part.one(to)

        return carry

    burst = FIRST * (BLOCK // LANES)
    lax.fori_loop(0, FIRST, whole, 0)
    lax.fori_loop(0, burst, send_parts, 0)
    lax.fori_loop(MIDDLE, LATE, every, 0)
    send_obs.arrive()
    total = total_of(ro)
    mine[...] = total
    ao[member] = total
    send_mine.start()
    lax.fori_loop(LATE, blocks, every, 0)
    lax.fori_loop(FIRST, blocks, whole, 0)
    send_obs.drain()
    send_mine.arrive()
    lane = lax.broadcasted_iota(jnp.int32, (4, LANES), 1)
    for n in range(groups):
        tile = ao[n]
        for g in range(shares):
            piece = tile if g == 0 else pltpu.roll(tile, LANES - width * g, 1)
            at = local * n + each * g
            flat[at : at + each, :] = jnp.where(lane < width, piece, 0.0)[0:each]
    predicted = flat[...]
    centre = jnp.sum(predicted, axis=0, keepdims=True) * (1.0 / members)
    anomaly = predicted - centre
    weight = observations[0:1]
    gram = mm_nt(anomaly, anomaly * weight)
    rhs = mm_nt(jnp.broadcast_to(weight * (observations[1:2] - centre), (8, LANES)), anomaly)
    size = members // 3
    top = jnp.concatenate([gram[0:size, 0:size], gram[2 * size :, 2 * size :]], axis=1)
    pieces = [top, gram[size:, 0 : 2 * size], rhs[:, 0:LANES]]
    pieces.append(jnp.concatenate([rhs[:, LANES:], jnp.zeros((8, 2 * LANES - members), F32)], axis=1))
    pieces.append(jnp.zeros((slabs * height - members - 16, LANES), F32))
    gpart[...] = jnp.concatenate(pieces, axis=0).reshape(slabs, height, LANES)
    far_first("slab", lambda to: pl.when(to < owners)(lambda: send_gram.one(to)))
    lax.fori_loop(burst, slabs, send_parts, 0)
    rs[slab] = part[slab]
    send_mine.drain()

    @pl.when(slab < owners)
    def _():
        gred[slab] = gpart[slab]
        send_gram.arrive()
        gall[slab] = total_of(gred)
        send_sum.start()

    def owned(wait):
        if owners == slabs:
            wait(owners - 1)
        else:
            pl.when(slab < owners)(lambda: wait(owners - 1))
            pl.when(slab >= owners)(lambda: wait(owners))

    owned(lambda n: send_gram.every(n).wait_send())
    send_fore.arrive()
    pile[member] = fore[member]
    for n in range(groups):
        flat[local * n : local * n + local, :] = pile[n]
    spread = flat[...]
    centre = jnp.sum(spread, axis=0, keepdims=True) * (1.0 / members)
    spread = spread - centre
    send_part.arrive()
    total = jnp.concatenate([total_of(rs), jnp.zeros((LANES - local, LANES), F32)], axis=0)
    turned[...] = total.T.reshape(groups, own, LANES)
    owned(lambda n: send_sum.every(n).wait_recv())
    send_own.start()
    got[member] = turned[member]
    packed = gall[...].reshape(slabs * height, LANES)
    rhs = jnp.concatenate(
        [packed[members : members + 1], packed[members + 8 : members + 9]], axis=1
    )[:, 0:members]
    mix = transform(packed[0:members], rhs, members)
    flat[...] = centre + mm(mix, spread)
    for n in range(groups):
        snd[n] = flat[local * n : local * n + local, :]
    send_back.start()
    back[member] = snd[member]
    send_own.arrive()
    total = jnp.zeros((own, 2 * LANES), F32)
    for n in range(groups):
        tile = jnp.concatenate([got[n], jnp.zeros((own, LANES), F32)], axis=1)
        total += tile if n == 0 else pltpu.roll(tile, local * n, 1)
    own_ref[...] = total[:, 0:members]
    for item in halos:
        item.wait_send()
    send_fore.drain()
    send_part.drain()
    pl.when(slab < owners)(send_sum.drain)
    send_own.drain()
    send_back.arrive()
    for i in range(rows):
        ret_ref[:, i, :] = back[i]
    send_back.drain()


def shards(
    fluid_head_start,
    conductivity_matrix,
    well_rates,
    cell_layer,
    pixel_coords,
    obs_index,
    obs_value,
    obs_sigma,
):
    local, rows, cols = fluid_head_start.shape
    groups = lax.axis_size("member")
    slabs = lax.axis_size("slab")
    members = local * groups
    pixels = pixel_coords.shape[1]
    observed = obs_index.shape[0]
    own = pixels // (groups * slabs)
    height = 256 // slabs
    place = pl.BlockSpec(memory_space=pltpu.VMEM)
    tall = rows + 2 * STEPS

    def f32(*shape):
        return pltpu.VMEM(shape, F32)

    def bf16(*shape):
        return pltpu.VMEM(shape, BF16)

    def pair(shape):
        return [pltpu.SemaphoreType.DMA(shape)] * 2

    body = lambda *refs: cycle_kernel(rows * slabs, *refs)
    arguments = (
        fluid_head_start,
        conductivity_matrix,
        well_rates,
        cell_layer,
        pixel_coords,
        obs_index[None],
        obs_value[None],
        obs_sigma[None],
    )
    returned, own_part = pl.pallas_call(
        body,
        name="cycle",
        out_shape=(
            jax.ShapeDtypeStruct((local, rows, cols), F32),
            jax.ShapeDtypeStruct((own, members), F32),
        ),
        in_specs=[pl.BlockSpec(memory_space=pltpu.HBM)] * 8,
        out_specs=(place, place),
        scratch_shapes=[
            f32(tall, local, cols),
            f32(tall, local, cols),
            f32(tall, 1, cols),
            f32(rows, local, cols),
            bf16(32, rows * cols),
            f32(rows, cols, LANES),
            f32(rows, cols, LANES),
            bf16(pixels // BLOCK, rows * cols, BLOCK),
            bf16(pixels // BLOCK, rows * cols, BLOCK),
            bf16(observed // BLOCK, rows * cols, BLOCK),
            bf16(observed // BLOCK, rows * cols, BLOCK),
            f32(2 * pixels // LANES, LANES),
            f32(8, observed),
            f32(2, pixels),
            bf16(64, rows * cols),
            f32(slabs, 4, LANES),
            f32(slabs, 4, LANES),
            f32(4, LANES),
            f32(groups, 4, LANES),
            f32(members, LANES),
            f32(slabs, local, LANES),
            f32(slabs, local, LANES),
            f32(groups, own, LANES),
            f32(groups, own, LANES),
            f32(slabs, height, LANES),
            f32(slabs, height, LANES),
            f32(slabs, height, LANES),
            f32(groups, local, cols),
            f32(groups, local, cols),
            f32(groups, local, cols),
            *pair((6,)),
            *(pair(()) * 8),
            *(pltpu.VMEM(value.shape, value.dtype) for value in arguments),
            pltpu.SemaphoreType.DMA((len(arguments),)),
        ],
        compiler_params=pltpu.CompilerParams(
            collective_id=0, has_side_effects=True, vmem_limit_bytes=52 * 1024 * 1024
        ),
    )(*(pltpu.with_memory_space_constraint(value, pltpu.HBM) for value in arguments))
    return (returned, own_part)


def solution(mesh):
    return jax.shard_map(
        shards,
        mesh=mesh,
        in_specs=(
            P("member", "slab", None),
            P("member", "slab", None),
            P("slab", None),
            P("slab", None),
            P(),
            P(),
            P(),
            P(),
        ),
        out_specs=(P("member", "slab", None), P(("member", "slab"), None)),
        check_vma=False,
    )
```

```python
import math

import jax
import jax.numpy as jnp
from jax import lax
from jax.experimental import pallas as pl
from jax.experimental.pallas import tpu as pltpu
from jax.sharding import PartitionSpec as P

STEPS = 4
time_step = 0.15
pixel_span = 64.0
top_depth = 2.0
F32 = jnp.float32
BF16 = jnp.bfloat16
HIGHEST = lax.Precision.HIGHEST
MESH = pl.DeviceIdType.MESH
BLOCK = 256
LANES = 128
EARLY = 3
MIDDLE = 9
LATE = 11
FIRST = 7
DEEP = 4


def split(value):
    high = value.astype(BF16)
    return high, (value - high.astype(F32)).astype(BF16)


def twice(value):
    return jnp.concatenate([value, value], axis=1)


def dot(a, b, dims):
    return lax.dot_general(a, b, (dims, ((), ())), precision=HIGHEST, preferred_element_type=F32)


def mm(a, b):
    return dot(a, b, ((1,), (0,)))


def mm_nt(a, b):
    return dot(a, b, ((1,), (1,)))


def inverse_factor(block):
    size = block.shape[0]
    wide = 2 * size
    count = size // 8
    sub = lax.broadcasted_iota(jnp.int32, (8, wide), 0)
    lane = lax.broadcasted_iota(jnp.int32, (8, wide), 1)

    def full(value):
        return jnp.broadcast_to(value, (8, wide))

    tiles = []
    for t in range(count):
        unit = jnp.where(lane == sub + (8 * t + size), 1.0, 0.0)
        tiles.append(jnp.concatenate([block[8 * t : 8 * t + 8], unit[:, size:]], axis=1))
    out = []
    for q in range(count):
        start = 8 * q
        cols = [
            [full(tiles[t][:, start + j : start + j + 1]) for t in range(q, count)] for j in range(8)
        ]
        lines = []
        top = tiles[q]
        pivots = None
        for k in range(0, 8, 2):
            left, right = cols[k], cols[k + 1]
            a = full(left[0][k : k + 1, :])
            b = full(left[0][k + 1 : k + 2, :])
            d = full(right[0][k + 1 : k + 2, :])
            det = a * d - b * b
            inv = 1.0 / det
            for j in range(k + 2, 8):
                u = full(left[0][j : j + 1, :])
                v = full(right[0][j : j + 1, :])
                p = (d * u - b * v) * inv
                r = (a * v - b * u) * inv
                cols[j] = [c - (x * p + y * r) for c, x, y in zip(cols[j], left, right)]
            u = full(top[k : k + 1, :])
            v = full(top[k + 1 : k + 2, :])
            p = (d * u - b * v) * inv
            r = (a * v - b * u) * inv
            lines += [p, r]
            ratio = 1.0 / a
            first = jnp.where(sub == k, a, det * ratio)
            pivots = first if k == 0 else jnp.where(sub >= k, first, pivots)
            step = left[0] * p + right[0] * r
            top = top - jnp.where(sub > k + 1, step, jnp.where(sub == k + 1, (b * ratio) * u, 0.0))
        out.append(top[:, size:] * lax.rsqrt(pivots)[:, size:])
        for t in range(q + 1, count):
            for k in range(8):
                tiles[t] = tiles[t] - cols[k][t - q] * lines[k]
    return jnp.concatenate(out, axis=0)


def transform(packed, rhs, members):
    size = members // 3
    row = lax.broadcasted_iota(jnp.int32, (members, 2 * size), 0)
    col = lax.broadcasted_iota(jnp.int32, (members, 2 * size), 1)
    gram = packed + jnp.where(row == col, members - 1.0, 0.0)
    corner = packed[0:size, size:] + jnp.where(row == col, members - 1.0, 0.0)[0:size, 0:size]
    l0 = inverse_factor(gram[0:size, 0:size])
    f10 = mm_nt(gram[size : 2 * size, 0:size], l0)
    s11 = gram[size : 2 * size, size:] - mm_nt(f10, f10)
    f20 = mm_nt(gram[2 * size :, 0:size], l0)
    s21 = gram[2 * size :, size:] - mm_nt(f20, f10)
    s22 = corner - mm_nt(f20, f20)
    z10 = mm(f10, l0)
    z20 = mm(f20, l0)
    l1 = inverse_factor(s11)
    f21 = mm_nt(s21, l1)
    l10 = -mm(l1, z10)
    l2 = inverse_factor(s22 - mm_nt(f21, f21))
    z2 = jnp.concatenate([-(z20 + mm(f21, l10)), -mm(f21, l1)], axis=1)
    l20 = mm(l2, z2)
    zero = jnp.zeros((size, size), F32)
    inverse = jnp.concatenate(
        [
            jnp.concatenate([l0, zero, zero], axis=1),
            jnp.concatenate([l10, l1, zero], axis=1),
            jnp.concatenate([l20, l2], axis=1),
        ],
        axis=0,
    )
    reduced = jnp.sum(inverse * rhs, axis=1, keepdims=True)
    weights = jnp.sum(inverse * reduced, axis=0, keepdims=True)
    return weights + math.sqrt(members - 1.0) * inverse


def advance(head, perm, source, open_first, open_last, first_row, rows):
    mobility = perm * (1.0 + 0.5 * jnp.tanh(head))
    last = head.shape[0] - 1
    cols = head.shape[2]
    flux = 0.5 * (mobility[1:] + mobility[:-1]) * (head[1:] - head[:-1])
    parts = [flux[i : i + 1] for i in range(last)]
    near, far = STEPS - 1 - first_row, STEPS - 1 + rows - first_row
    parts[near] = parts[near] * open_first
    parts[far] = parts[far] * open_last
    flux = jnp.concatenate(parts, axis=0)
    inner = head[1:-1]
    own = mobility[1:-1]
    lane = lax.broadcasted_iota(jnp.int32, inner.shape, 2)
    along = 0.5 * (jnp.roll(own, -1, axis=2) + own) * (jnp.roll(inner, -1, axis=2) - inner)
    along = jnp.where(lane < cols - 1, along, 0.0)
    back = jnp.where(lane > 0, jnp.roll(along, 1, axis=2), 0.0)
    inflow = (flux[1:] - flux[:-1]) + (along - back)
    return inner + time_step * (inflow + source[1:-1])


def cycle_kernel(total_rows, *refs):
    arguments, staged, staged_s = refs[:8], refs[-9:-1], refs[-1]
    refs = refs[:-9]
    head_ref, cond_ref, well_ref, lay_ref, pc_ref, oi_ref, ov_ref, os_ref = staged
    ret_ref, own_ref = refs[8:10]
    hx, cx, wx, fore, w_ref, h2_ref, vh_ref, khi, klo, ohi, olo, place, where = refs[10:23]
    pcs, wo_ref, po, ro, mine, ao, flat, part, rs, turned, got, gpart, gred, gall, pile, snd, back = refs[23:40]
    halo_s, halo_r, out_s, out_r, ro_s, ro_r, ao_s, ao_r = refs[40:48]
    g1_s, g1_r, rs_s, rs_r, g2_s, g2_r, tu_s, tu_r, rt_s, rt_r = refs[48:]

    slab, member = lax.axis_index("slab"), lax.axis_index("member")
    slabs, groups = lax.axis_size("slab"), lax.axis_size("member")
    local, rows, cols = head_ref.shape
    members = local * groups
    pixels = pc_ref.shape[1]
    observed = oi_ref.shape[1]
    blocks, obs_blocks = pixels // BLOCK, observed // BLOCK
    row_pitch, col_pitch = pixel_span / total_rows, pixel_span / cols
    volume = pixel_span * pixel_span / (total_rows * cols)

    def other(i, axis):
        me, n = (slab, slabs) if axis == "slab" else (member, groups)
        return lax.rem(me + i, n)

    def peers(axis, body):
        n = slabs if axis == "slab" else groups

        def step(i, carry):
            body(other(i, axis))
            return carry

        lax.fori_loop(1, n, step, 0)

    def far_first(axis, body):
        if axis == "member":
            inner = groups // DEEP
            across = [lax.rem(member // DEEP + i, inner) * DEEP for i in range(inner)]
            along = [lax.rem(member + i, DEEP) for i in range(DEEP)]
            cores = [0]
        else:
            inner = slabs // (2 * DEEP)
            across = [lax.rem(slab // (2 * DEEP) + i, inner) * (2 * DEEP) for i in range(inner)]
            along = [lax.rem(slab // 2 + i, DEEP) * 2 for i in range(DEEP)]
            cores = [lax.rem(slab, 2), lax.rem(slab + 1, 2)]
        for dz in (2, 1, 3, 0):
            for i in range(inner):
                for c, core in enumerate(cores):
                    if dz or i or c:
                        body(across[i] + along[dz] + core)

    def copy(src, dst, ssem, rsem, axis, to):
        return pltpu.make_async_remote_copy(
            src_ref=src,
            dst_ref=dst,
            send_sem=ssem,
            recv_sem=rsem,
            device_id={axis: to},
            device_id_type=MESH,
        )

    class Exchange:
        def __init__(self, axis, src, dst, ssem, rsem):
            self.axis, self.src, self.dst, self.ssem, self.rsem = axis, src, dst, ssem, rsem
            self.me = slab if axis == "slab" else member

        def one(self, to):
            copy(self.src(to), self.dst.at[self.me], self.ssem, self.rsem, self.axis, to).start()

        def start(self):
            far_first(self.axis, self.one)

        def every(self, n=None):
            part = self.dst.at[pl.ds(0, n or self.dst.shape[0] - 1)]
            return copy(part, part, self.ssem, self.rsem, self.axis, other(1, self.axis))

        def arrive(self):
            self.every().wait_recv()

        def drain(self):
            self.every().wait_send()

    height = gpart.shape[1]
    owners = (members + 16 + height - 1) // height

    def total_of(ref):
        value = ref[0]
        for n in range(1, ref.shape[0]):
            value += ref[n]
        return value

    send_fore = Exchange("member", lambda to: fore.at[to], pile, out_s, out_r)
    send_obs = Exchange("slab", lambda to: po.at[to], ro, ro_s, ro_r)
    send_mine = Exchange("member", lambda to: mine, ao, ao_s, ao_r)
    send_gram = Exchange("slab", lambda to: gpart.at[to], gred, g1_s, g1_r)
    send_part = Exchange("slab", lambda to: part.at[to], rs, rs_s, rs_r)
    send_sum = Exchange("slab", lambda to: gall.at[slab], gall, g2_s, g2_r)
    send_own = Exchange("member", lambda to: turned.at[to], got, tu_s, tu_r)
    send_back = Exchange("member", lambda to: snd.at[to], back, rt_s, rt_r)

    loads = [
        pltpu.make_async_copy(src, dst, staged_s.at[n])
        for n, (src, dst) in enumerate(zip(arguments, staged))
    ]
    for item in loads:
        item.start()
    barrier = pltpu.get_barrier_semaphore()
    for axis in ("slab", "member"):
        peers(
            axis,
            lambda to: pl.semaphore_signal(barrier, inc=1, device_id={axis: to}, device_id_type=MESH),
        )

    for item in loads:
        item.wait()
    for i in range(rows):
        hx[STEPS + i] = head_ref[:, i, :]
        cx[STEPS + i] = cond_ref[:, i, :]
        wx[STEPS + i] = well_ref[i : i + 1, :]
    depth = top_depth + lay_ref[...].astype(F32)
    depth = jnp.concatenate([depth, jnp.zeros((cols - rows, cols), F32)], axis=0).T
    for i in range(rows):
        column = depth[:, i : i + 1]
        h2_ref[i] = jnp.broadcast_to(column * column, (cols, LANES))
        vh_ref[i] = jnp.broadcast_to(volume * column, (cols, LANES))
    cell_y = (lax.broadcasted_iota(jnp.int32, (cols, BLOCK), 0).astype(F32) + 0.5) * col_pitch
    first = (slab * rows).astype(F32)

    def evaluate(coords_ref, high_ref, low_ref):
        def step(n, carry):
            b = lax.rem(n + slab // 2, coords_ref.shape[1] // BLOCK)
            at = pl.multiple_of(b * BLOCK, BLOCK)
            coords = coords_ref[0:2, pl.ds(at, BLOCK)].astype(F32)
            delta_y = cell_y - coords[1:2]
            dy2 = delta_y * delta_y
            for i in range(rows):
                delta_x = (first + (i + 0.5)) * row_pitch - coords[0:1]
                radius = (dy2 + delta_x * delta_x) + twice(h2_ref[i])
                inv = lax.rsqrt(radius)
                high, low = split(twice(vh_ref[i]) * (inv * inv * inv))
                high_ref[b, cols * i : cols * i + cols, :] = high
                low_ref[b, cols * i : cols * i + cols, :] = low
            return carry

        return step

    groups_of = pixels // LANES
    for c in range(2):
        for n in range(groups_of):
            place[groups_of * c + n : groups_of * c + n + 1, :] = pc_ref[
                c : c + 1, LANES * n : LANES * n + LANES
            ].astype(F32)
    own = LANES // groups
    near = slabs * own // LANES
    line = lax.broadcasted_iota(jnp.int32, (groups, LANES), 0)
    lane = lax.broadcasted_iota(jnp.int32, (groups, LANES), 1)
    widen = jnp.where(lane // own == line, 1.0, 0.0).astype(BF16)
    line = lax.broadcasted_iota(jnp.int32, (LANES, LANES), 0)
    lane = lax.broadcasted_iota(jnp.int32, (LANES, LANES), 1)
    same = lax.rem(line, own) == lax.rem(lane, own)
    for c in range(2):
        for h in range(near):
            table = place[pl.ds(groups_of * c + h, groups, stride=near), :].astype(BF16)
            wide = lax.dot_general(
                table, widen, (((0,), (0,)), ((), ())), preferred_element_type=F32
            )
            wide = jnp.sum(jnp.where(same, wide, 0.0).reshape(LANES // own, own, LANES), axis=1)
            for n in range(LANES // own):
                at = (h * (LANES // own) + n) * LANES
                pcs[c : c + 1, at : at + LANES] = wide[n : n + 1]
    high_part, low_part = oi_ref[...] // LANES, lax.rem(oi_ref[...], LANES)
    line = lax.broadcasted_iota(jnp.int32, (groups_of, observed), 0)
    pick = jnp.where(line == high_part, 1.0, 0.0).astype(BF16)
    spot = lax.broadcasted_iota(jnp.int32, (LANES, observed), 0) == low_part
    for c in range(2):
        table = place[groups_of * c : groups_of * c + groups_of, :].astype(BF16)
        found = lax.dot_general(table, pick, (((0,), (0,)), ((), ())), preferred_element_type=F32)
        where[c : c + 1, :] = jnp.sum(jnp.where(spot, found, 0.0), axis=0, keepdims=True)
    lax.fori_loop(0, obs_blocks, evaluate(where, ohi, olo), 0)
    every = evaluate(pcs, khi, klo)
    lax.fori_loop(0, EARLY, every, 0)

    pl.semaphore_wait(barrier, slabs - 1 + groups - 1)

    up, down = other(1, "slab"), other(slabs - 1, "slab")
    halos = []
    for n, grown in enumerate((hx, cx, wx)):
        for side, (frm, at, to) in enumerate(((rows, 0, up), (STEPS, rows + STEPS, down))):
            halos.append(
                copy(
                    grown.at[pl.ds(frm, STEPS)],
                    grown.at[pl.ds(at, STEPS)],
                    halo_s.at[2 * n + side],
                    halo_r.at[2 * n + side],
                    "slab",
                    to,
                )
            )
    for item in halos:
        item.start()
    lax.fori_loop(EARLY, MIDDLE, every, 0)
    width = observed // slabs
    inverse_var = 1.0 / (os_ref[...] * os_ref[...])
    first_line = lax.broadcasted_iota(jnp.int32, (8, observed), 0) == 0
    observations = jnp.where(first_line, inverse_var, ov_ref[...])
    observations = pltpu.roll(observations, lax.rem(observed - width * slab, observed), 1)
    inside = lax.broadcasted_iota(jnp.int32, (8, LANES), 1) < width
    observations = jnp.where(inside, observations[:, 0:LANES], 0.0)

    for item in halos:
        item.wait_recv()
    head, perm, source = hx[...], cx[...], wx[...]
    open_first = jnp.where(slab == 0, 0.0, 1.0)
    open_last = jnp.where(slab == slabs - 1, 0.0, 1.0)
    for k in range(STEPS):
        head = advance(head, perm, source, open_first, open_last, k, rows)
        perm, source = perm[1:-1], source[1:-1]
    fore[...] = head
    w_ref[...] = jnp.zeros_like(w_ref)
    for i in range(rows):
        high, low = split(head[i])
        w_ref[0:local, cols * i : cols * i + cols] = high
        w_ref[16 : 16 + local, cols * i : cols * i + cols] = low

    shares = LANES // width
    each = local // shares
    line = lax.broadcasted_iota(jnp.int32, (64, 32), 0)
    col = lax.broadcasted_iota(jnp.int32, (64, 32), 1)
    wanted = lax.rem(line // 8, 4) * each + lax.rem(line, 8) + (line // 32) * 16
    valid = lax.rem(line, 8) < each
    gather = jnp.where(valid & (col == wanted), 1.0, 0.0).astype(BF16)
    wo_ref[...] = jnp.dot(gather, w_ref[...], preferred_element_type=F32).astype(BF16)
    lane = lax.broadcasted_iota(jnp.int32, (8, LANES), 1) // width
    order = [lax.rem(n + slab // (slabs // obs_blocks), obs_blocks) for n in range(obs_blocks)]

    def seen(b):
        total = jnp.dot(wo_ref[...], ohi[b], preferred_element_type=F32)
        total += jnp.dot(wo_ref[...], olo[b], preferred_element_type=F32)
        return total[0:32] + total[32:64]

    ahead = seen(order[0])
    for n, b in enumerate(order):
        total = ahead
        if n + 1 < obs_blocks:
            ahead = seen(order[n + 1])
        for half in range(BLOCK // LANES):
            block = total[:, LANES * half : LANES * half + LANES]
            for u in range(shares):
                chunk = None
                for g in range(shares):
                    piece = pltpu.roll(block[8 * g : 8 * g + 8], (width * (g - u)) % LANES, 1)
                    chunk = piece if g == 0 else jnp.where(lane == g, piece, chunk)
                po[(b * (BLOCK // LANES) + half) * shares + u] = chunk[0:4]
        count = slabs // obs_blocks

        def send(i, carry, b=b):
            to = b * count + lax.rem(i + slab, count)

            @pl.when(to != slab)
            def _():
                send_obs.one(to)

            return carry

        lax.fori_loop(0, count, send, 0)
    send_fore.start()
    ro[slab] = po[slab]

    def whole(n, carry):
        b = lax.rem(n + slab // 2, blocks)
        total = jnp.dot(w_ref[...], khi[b], preferred_element_type=F32)
        total += jnp.dot(w_ref[...], klo[b], preferred_element_type=F32)
        total = total[0:16] + total[16:32]
        for half in range(BLOCK // LANES):
            part[b * (BLOCK // LANES) + half] = total[0:local, LANES * half : LANES * half + LANES]
        return carry

    def send_parts(n, carry):
        to = lax.rem(n + (slab // 2) * (BLOCK // LANES), slabs)

        @pl.when(to != slab)
        def _():
            send_part.one(to)

        return carry

    burst = FIRST * (BLOCK // LANES)
    lax.fori_loop(0, FIRST, whole, 0)
    lax.fori_loop(0, burst, send_parts, 0)
    lax.fori_loop(MIDDLE, LATE, every, 0)
    send_obs.arrive()
    total = total_of(ro)
    mine[...] = total
    ao[member] = total
    send_mine.start()
    lax.fori_loop(LATE, blocks, every, 0)
    lax.fori_loop(FIRST, blocks, whole, 0)
    send_obs.drain()
    send_mine.arrive()
    lane = lax.broadcasted_iota(jnp.int32, (4, LANES), 1)
    for n in range(groups):
        tile = ao[n]
        for g in range(shares):
            piece = tile if g == 0 else pltpu.roll(tile, LANES - width * g, 1)
            at = local * n + each * g
            flat[at : at + each, :] = jnp.where(lane < width, piece, 0.0)[0:each]
    predicted = flat[...]
    centre = jnp.sum(predicted, axis=0, keepdims=True) * (1.0 / members)
    anomaly = predicted - centre
    weight = observations[0:1]
    gram = mm_nt(anomaly, anomaly * weight)
    rhs = mm_nt(jnp.broadcast_to(weight * (observations[1:2] - centre), (8, LANES)), anomaly)
    size = members // 3
    top = jnp.concatenate([gram[0:size, 0:size], gram[2 * size :, 2 * size :]], axis=1)
    pieces = [top, gram[size:, 0 : 2 * size], rhs[:, 0:LANES]]
    pieces.append(jnp.concatenate([rhs[:, LANES:], jnp.zeros((8, 2 * LANES - members), F32)], axis=1))
    pieces.append(jnp.zeros((slabs * height - members - 16, LANES), F32))
    gpart[...] = jnp.concatenate(pieces, axis=0).reshape(slabs, height, LANES)
    far_first("slab", lambda to: pl.when(to < owners)(lambda: send_gram.one(to)))
    lax.fori_loop(burst, slabs, send_parts, 0)
    rs[slab] = part[slab]
    send_mine.drain()

    @pl.when(slab < owners)
    def _():
        gred[slab] = gpart[slab]
        send_gram.arrive()
        gall[slab] = total_of(gred)
        send_sum.start()

    def owned(wait):
        if owners == slabs:
            wait(owners - 1)
        else:
            pl.when(slab < owners)(lambda: wait(owners - 1))
            pl.when(slab >= owners)(lambda: wait(owners))

    owned(lambda n: send_gram.every(n).wait_send())
    send_fore.arrive()
    pile[member] = fore[member]
    for n in range(groups):
        flat[local * n : local * n + local, :] = pile[n]
    spread = flat[...]
    centre = jnp.sum(spread, axis=0, keepdims=True) * (1.0 / members)
    spread = spread - centre
    send_part.arrive()
    total = jnp.concatenate([total_of(rs), jnp.zeros((LANES - local, LANES), F32)], axis=0)
    turned[...] = total.T.reshape(groups, own, LANES)
    owned(lambda n: send_sum.every(n).wait_recv())
    send_own.start()
    got[member] = turned[member]
    packed = gall[...].reshape(slabs * height, LANES)
    rhs = jnp.concatenate(
        [packed[members : members + 1], packed[members + 8 : members + 9]], axis=1
    )[:, 0:members]
    mix = transform(packed[0:members], rhs, members)
    flat[...] = centre + mm(mix, spread)
    for n in range(groups):
        snd[n] = flat[local * n : local * n + local, :]
    send_back.start()
    back[member] = snd[member]
    send_own.arrive()
    total = jnp.zeros((own, 2 * LANES), F32)
    for n in range(groups):
        tile = jnp.concatenate([got[n], jnp.zeros((own, LANES), F32)], axis=1)
        total += tile if n == 0 else pltpu.roll(tile, local * n, 1)
    own_ref[...] = total[:, 0:members]
    for item in halos:
        item.wait_send()
    send_fore.drain()
    send_part.drain()
    pl.when(slab < owners)(send_sum.drain)
    send_own.drain()
    send_back.arrive()
    for i in range(rows):
        ret_ref[:, i, :] = back[i]
    send_back.drain()


def shards(
    fluid_head_start,
    conductivity_matrix,
    well_rates,
    cell_layer,
    pixel_coords,
    obs_index,
    obs_value,
    obs_sigma,
):
    local, rows, cols = fluid_head_start.shape
    groups = lax.axis_size("member")
    slabs = lax.axis_size("slab")
    members = local * groups
    pixels = pixel_coords.shape[1]
    observed = obs_index.shape[0]
    own = pixels // (groups * slabs)
    height = 256 // slabs
    place = pl.BlockSpec(memory_space=pltpu.VMEM)
    tall = rows + 2 * STEPS

    def f32(*shape):
        return pltpu.VMEM(shape, F32)

    def bf16(*shape):
        return pltpu.VMEM(shape, BF16)

    def pair(shape):
        return [pltpu.SemaphoreType.DMA(shape)] * 2

    body = lambda *refs: cycle_kernel(rows * slabs, *refs)
    arguments = (
        fluid_head_start,
        conductivity_matrix,
        well_rates,
        cell_layer,
        pixel_coords,
        obs_index[None],
        obs_value[None],
        obs_sigma[None],
    )
    returned, own_part = pl.pallas_call(
        body,
        name="cycle",
        out_shape=(
            jax.ShapeDtypeStruct((local, rows, cols), F32),
            jax.ShapeDtypeStruct((own, members), F32),
        ),
        in_specs=[pl.BlockSpec(memory_space=pltpu.HBM)] * 8,
        out_specs=(place, place),
        scratch_shapes=[
            f32(tall, local, cols),
            f32(tall, local, cols),
            f32(tall, 1, cols),
            f32(rows, local, cols),
            bf16(32, rows * cols),
            f32(rows, cols, LANES),
            f32(rows, cols, LANES),
            bf16(pixels // BLOCK, rows * cols, BLOCK),
            bf16(pixels // BLOCK, rows * cols, BLOCK),
            bf16(observed // BLOCK, rows * cols, BLOCK),
            bf16(observed // BLOCK, rows * cols, BLOCK),
            f32(2 * pixels // LANES, LANES),
            f32(8, observed),
            f32(2, pixels),
            bf16(64, rows * cols),
            f32(slabs, 4, LANES),
            f32(slabs, 4, LANES),
            f32(4, LANES),
            f32(groups, 4, LANES),
            f32(members, LANES),
            f32(slabs, local, LANES),
            f32(slabs, local, LANES),
            f32(groups, own, LANES),
            f32(groups, own, LANES),
            f32(slabs, height, LANES),
            f32(slabs, height, LANES),
            f32(slabs, height, LANES),
            f32(groups, local, cols),
            f32(groups, local, cols),
            f32(groups, local, cols),
            *pair((6,)),
            *(pair(()) * 8),
            *(pltpu.VMEM(value.shape, value.dtype) for value in arguments),
            pltpu.SemaphoreType.DMA((len(arguments),)),
        ],
        compiler_params=pltpu.CompilerParams(
            collective_id=0, has_side_effects=True, vmem_limit_bytes=52 * 1024 * 1024
        ),
    )(*(pltpu.with_memory_space_constraint(value, pltpu.HBM) for value in arguments))
    return (returned, own_part)


def solution(mesh):
    return jax.shard_map(
        shards,
        mesh=mesh,
        in_specs=(
            P("member", "slab", None),
            P("member", "slab", None),
            P("slab", None),
            P("slab", None),
            P(),
            P(),
            P(),
            P(),
        ),
        out_specs=(P("member", "slab", None), P(("member", "slab"), None)),
        check_vma=False,
    )
```

```python
import math

import jax
import jax.numpy as jnp
from jax import lax
from jax.experimental import pallas as pl
from jax.experimental.pallas import tpu as pltpu
from jax.sharding import PartitionSpec as P

STEPS = 4
time_step = 0.15
pixel_span = 64.0
top_depth = 2.0
F32 = jnp.float32
BF16 = jnp.bfloat16
HIGHEST = lax.Precision.HIGHEST
MESH = pl.DeviceIdType.MESH
BLOCK = 256
LANES = 128
EARLY = 3
MIDDLE = 8
LATE = 10
FIRST = 7
SECOND = 14
DEEP = 4


def split(value):
    high = value.astype(BF16)
    return high, (value - high.astype(F32)).astype(BF16)


def twice(value):
    return jnp.concatenate([value, value], axis=1)


def dot(a, b, dims):
    return lax.dot_general(a, b, (dims, ((), ())), precision=HIGHEST, preferred_element_type=F32)


def mm(a, b):
    return dot(a, b, ((1,), (0,)))


def mm_nt(a, b):
    return dot(a, b, ((1,), (1,)))


def inverse_factor(block):
    size = block.shape[0]
    wide = 2 * size
    count = size // 8
    sub = lax.broadcasted_iota(jnp.int32, (8, wide), 0)
    lane = lax.broadcasted_iota(jnp.int32, (8, wide), 1)

    def full(value):
        return jnp.broadcast_to(value, (8, wide))

    tiles = []
    for t in range(count):
        unit = jnp.where(lane == sub + (8 * t + size), 1.0, 0.0)
        tiles.append(jnp.concatenate([block[8 * t : 8 * t + 8], unit[:, size:]], axis=1))
    out = []
    for q in range(count):
        start = 8 * q
        cols = [
            [full(tiles[t][:, start + j : start + j + 1]) for t in range(q, count)] for j in range(8)
        ]
        lines = []
        top = tiles[q]
        pivots = None
        for k in range(0, 8, 2):
            left, right = cols[k], cols[k + 1]
            a = full(left[0][k : k + 1, :])
            b = full(left[0][k + 1 : k + 2, :])
            d = full(right[0][k + 1 : k + 2, :])
            det = a * d - b * b
            inv = 1.0 / det
            for j in range(k + 2, 8):
                u = full(left[0][j : j + 1, :])
                v = full(right[0][j : j + 1, :])
                p = (d * u - b * v) * inv
                r = (a * v - b * u) * inv
                cols[j] = [c - (x * p + y * r) for c, x, y in zip(cols[j], left, right)]
            u = full(top[k : k + 1, :])
            v = full(top[k + 1 : k + 2, :])
            p = (d * u - b * v) * inv
            r = (a * v - b * u) * inv
            lines += [p, r]
            ratio = 1.0 / a
            first = jnp.where(sub == k, a, det * ratio)
            pivots = first if k == 0 else jnp.where(sub >= k, first, pivots)
            step = left[0] * p + right[0] * r
            top = top - jnp.where(sub > k + 1, step, jnp.where(sub == k + 1, (b * ratio) * u, 0.0))
        out.append(top[:, size:] * lax.rsqrt(pivots)[:, size:])
        for t in range(q + 1, count):
            for k in range(8):
                tiles[t] = tiles[t] - cols[k][t - q] * lines[k]
    return jnp.concatenate(out, axis=0)


def transform(packed, rhs, members):
    size = members // 3
    row = lax.broadcasted_iota(jnp.int32, (members, 2 * size), 0)
    col = lax.broadcasted_iota(jnp.int32, (members, 2 * size), 1)
    gram = packed + jnp.where(row == col, members - 1.0, 0.0)
    corner = packed[0:size, size:] + jnp.where(row == col, members - 1.0, 0.0)[0:size, 0:size]
    l0 = inverse_factor(gram[0:size, 0:size])
    f10 = mm_nt(gram[size : 2 * size, 0:size], l0)
    s11 = gram[size : 2 * size, size:] - mm_nt(f10, f10)
    f20 = mm_nt(gram[2 * size :, 0:size], l0)
    s21 = gram[2 * size :, size:] - mm_nt(f20, f10)
    s22 = corner - mm_nt(f20, f20)
    z10 = mm(f10, l0)
    z20 = mm(f20, l0)
    l1 = inverse_factor(s11)
    f21 = mm_nt(s21, l1)
    l10 = -mm(l1, z10)
    l2 = inverse_factor(s22 - mm_nt(f21, f21))
    z2 = jnp.concatenate([-(z20 + mm(f21, l10)), -mm(f21, l1)], axis=1)
    l20 = mm(l2, z2)
    zero = jnp.zeros((size, size), F32)
    inverse = jnp.concatenate(
        [
            jnp.concatenate([l0, zero, zero], axis=1),
            jnp.concatenate([l10, l1, zero], axis=1),
            jnp.concatenate([l20, l2], axis=1),
        ],
        axis=0,
    )
    reduced = jnp.sum(inverse * rhs, axis=1, keepdims=True)
    weights = jnp.sum(inverse * reduced, axis=0, keepdims=True)
    return weights + math.sqrt(members - 1.0) * inverse


def advance(head, perm, source, open_first, open_last, first_row, rows):
    mobility = perm * (1.0 + 0.5 * jnp.tanh(head))
    last = head.shape[0] - 1
    cols = head.shape[2]
    flux = 0.5 * (mobility[1:] + mobility[:-1]) * (head[1:] - head[:-1])
    parts = [flux[i : i + 1] for i in range(last)]
    near, far = STEPS - 1 - first_row, STEPS - 1 + rows - first_row
    parts[near] = parts[near] * open_first
    parts[far] = parts[far] * open_last
    flux = jnp.concatenate(parts, axis=0)
    inner = head[1:-1]
    own = mobility[1:-1]
    lane = lax.broadcasted_iota(jnp.int32, inner.shape, 2)
    along = 0.5 * (jnp.roll(own, -1, axis=2) + own) * (jnp.roll(inner, -1, axis=2) - inner)
    along = jnp.where(lane < cols - 1, along, 0.0)
    back = jnp.where(lane > 0, jnp.roll(along, 1, axis=2), 0.0)
    inflow = (flux[1:] - flux[:-1]) + (along - back)
    return inner + time_step * (inflow + source[1:-1])


def cycle_kernel(total_rows, *refs):
    arguments, staged, staged_s = refs[:8], refs[-9:-1], refs[-1]
    refs = refs[:-9]
    head_ref, cond_ref, well_ref, lay_ref, pc_ref, oi_ref, ov_ref, os_ref = staged
    ret_ref, own_ref = refs[8:10]
    hx, cx, wx, fore, w_ref, h2_ref, vh_ref, khi, klo, ohi, olo, place, where = refs[10:23]
    pcs, wo_ref, po, ro, mine, ao, flat, part, rs, turned, got, gpart, gred, gall, pile, snd, back = refs[23:40]
    halo_s, halo_r, out_s, out_r, ro_s, ro_r, ao_s, ao_r = refs[40:48]
    g1_s, g1_r, rs_s, rs_r, g2_s, g2_r, tu_s, tu_r, rt_s, rt_r = refs[48:]

    slab, member = lax.axis_index("slab"), lax.axis_index("member")
    slabs, groups = lax.axis_size("slab"), lax.axis_size("member")
    local, rows, cols = head_ref.shape
    members = local * groups
    pixels = pc_ref.shape[1]
    observed = oi_ref.shape[1]
    blocks, obs_blocks = pixels // BLOCK, observed // BLOCK
    row_pitch, col_pitch = pixel_span / total_rows, pixel_span / cols
    volume = pixel_span * pixel_span / (total_rows * cols)

    def other(i, axis):
        me, n = (slab, slabs) if axis == "slab" else (member, groups)
        return lax.rem(me + i, n)

    def peers(axis, body):
        n = slabs if axis == "slab" else groups

        def step(i, carry):
            body(other(i, axis))
            return carry

        lax.fori_loop(1, n, step, 0)

    def far_first(axis, body):
        if axis == "member":
            inner = groups // DEEP
            across = [lax.rem(member // DEEP + i, inner) * DEEP for i in range(inner)]
            along = [lax.rem(member + i, DEEP) for i in range(DEEP)]
            cores = [0]
        else:
            inner = slabs // (2 * DEEP)
            across = [lax.rem(slab // (2 * DEEP) + i, inner) * (2 * DEEP) for i in range(inner)]
            along = [lax.rem(slab // 2 + i, DEEP) * 2 for i in range(DEEP)]
            cores = [lax.rem(slab, 2), lax.rem(slab + 1, 2)]
        for dz in (2, 1, 3, 0):
            for i in range(inner):
                for c, core in enumerate(cores):
                    if dz or i or c:
                        body(across[i] + along[dz] + core)

    def copy(src, dst, ssem, rsem, axis, to):
        return pltpu.make_async_remote_copy(
            src_ref=src,
            dst_ref=dst,
            send_sem=ssem,
            recv_sem=rsem,
            device_id={axis: to},
            device_id_type=MESH,
        )

    class Exchange:
        def __init__(self, axis, src, dst, ssem, rsem):
            self.axis, self.src, self.dst, self.ssem, self.rsem = axis, src, dst, ssem, rsem
            self.me = slab if axis == "slab" else member

        def one(self, to):
            copy(self.src(to), self.dst.at[self.me], self.ssem, self.rsem, self.axis, to).start()

        def start(self):
            far_first(self.axis, self.one)

        def every(self, n=None):
            part = self.dst.at[pl.ds(0, n or self.dst.shape[0] - 1)]
            return copy(part, part, self.ssem, self.rsem, self.axis, other(1, self.axis))

        def arrive(self):
            self.every().wait_recv()

        def drain(self):
            self.every().wait_send()

    height = gpart.shape[1]
    owners = (members + 16 + height - 1) // height

    def total_of(ref):
        value = ref[0]
        for n in range(1, ref.shape[0]):
            value += ref[n]
        return value

    send_fore = Exchange("member", lambda to: fore.at[to], pile, out_s, out_r)
    send_obs = Exchange("slab", lambda to: po.at[to], ro, ro_s, ro_r)
    send_mine = Exchange("member", lambda to: mine, ao, ao_s, ao_r)
    send_gram = Exchange("slab", lambda to: gpart.at[to], gred, g1_s, g1_r)
    send_part = Exchange("slab", lambda to: part.at[to], rs, rs_s, rs_r)
    send_sum = Exchange("slab", lambda to: gall.at[slab], gall, g2_s, g2_r)
    send_own = Exchange("member", lambda to: turned.at[to], got, tu_s, tu_r)
    send_back = Exchange("member", lambda to: snd.at[to], back, rt_s, rt_r)

    loads = [
        pltpu.make_async_copy(src, dst, staged_s.at[n])
        for n, (src, dst) in enumerate(zip(arguments, staged))
    ]
    for item in loads:
        item.start()
    barrier = pltpu.get_barrier_semaphore()
    for axis in ("slab", "member"):
        peers(
            axis,
            lambda to: pl.semaphore_signal(barrier, inc=1, device_id={axis: to}, device_id_type=MESH),
        )

    for item in loads:
        item.wait()
    for i in range(rows):
        hx[STEPS + i] = head_ref[:, i, :]
        cx[STEPS + i] = cond_ref[:, i, :]
        wx[STEPS + i] = well_ref[i : i + 1, :]
    depth = top_depth + lay_ref[...].astype(F32)
    depth = jnp.concatenate([depth, jnp.zeros((cols - rows, cols), F32)], axis=0).T
    for i in range(rows):
        column = depth[:, i : i + 1]
        h2_ref[i] = jnp.broadcast_to(column * column, (cols, LANES))
        vh_ref[i] = jnp.broadcast_to(volume * column, (cols, LANES))
    cell_y = (lax.broadcasted_iota(jnp.int32, (cols, BLOCK), 0).astype(F32) + 0.5) * col_pitch
    first = (slab * rows).astype(F32)

    def evaluate(coords_ref, high_ref, low_ref):
        def step(n, carry):
            b = lax.rem(n + slab // 2, coords_ref.shape[1] // BLOCK)
            at = pl.multiple_of(b * BLOCK, BLOCK)
            coords = coords_ref[0:2, pl.ds(at, BLOCK)].astype(F32)
            delta_y = cell_y - coords[1:2]
            dy2 = delta_y * delta_y
            for i in range(rows):
                delta_x = (first + (i + 0.5)) * row_pitch - coords[0:1]
                radius = (dy2 + delta_x * delta_x) + twice(h2_ref[i])
                inv = lax.rsqrt(radius)
                high, low = split(twice(vh_ref[i]) * (inv * inv * inv))
                high_ref[b, cols * i : cols * i + cols, :] = high
                low_ref[b, cols * i : cols * i + cols, :] = low
            return carry

        return step

    groups_of = pixels // LANES
    for c in range(2):
        for n in range(groups_of):
            place[groups_of * c + n : groups_of * c + n + 1, :] = pc_ref[
                c : c + 1, LANES * n : LANES * n + LANES
            ].astype(F32)
    own = LANES // groups
    near = slabs * own // LANES
    line = lax.broadcasted_iota(jnp.int32, (groups, LANES), 0)
    lane = lax.broadcasted_iota(jnp.int32, (groups, LANES), 1)
    widen = jnp.where(lane // own == line, 1.0, 0.0).astype(BF16)
    line = lax.broadcasted_iota(jnp.int32, (LANES, LANES), 0)
    lane = lax.broadcasted_iota(jnp.int32, (LANES, LANES), 1)
    same = lax.rem(line, own) == lax.rem(lane, own)
    for c in range(2):
        for h in range(near):
            table = place[pl.ds(groups_of * c + h, groups, stride=near), :].astype(BF16)
            wide = lax.dot_general(
                table, widen, (((0,), (0,)), ((), ())), preferred_element_type=F32
            )
            wide = jnp.sum(jnp.where(same, wide, 0.0).reshape(LANES // own, own, LANES), axis=1)
            for n in range(LANES // own):
                at = (h * (LANES // own) + n) * LANES
                pcs[c : c + 1, at : at + LANES] = wide[n : n + 1]
    high_part, low_part = oi_ref[...] // LANES, lax.rem(oi_ref[...], LANES)
    line = lax.broadcasted_iota(jnp.int32, (groups_of, observed), 0)
    pick = jnp.where(line == high_part, 1.0, 0.0).astype(BF16)
    spot = lax.broadcasted_iota(jnp.int32, (LANES, observed), 0) == low_part
    for c in range(2):
        table = place[groups_of * c : groups_of * c + groups_of, :].astype(BF16)
        found = lax.dot_general(table, pick, (((0,), (0,)), ((), ())), preferred_element_type=F32)
        where[c : c + 1, :] = jnp.sum(jnp.where(spot, found, 0.0), axis=0, keepdims=True)
    lax.fori_loop(0, obs_blocks, evaluate(where, ohi, olo), 0)
    every = evaluate(pcs, khi, klo)
    lax.fori_loop(0, EARLY, every, 0)

    pl.semaphore_wait(barrier, slabs - 1 + groups - 1)

    up, down = other(1, "slab"), other(slabs - 1, "slab")
    halos = []
    for n, grown in enumerate((hx, cx, wx)):
        for side, (frm, at, to) in enumerate(((rows, 0, up), (STEPS, rows + STEPS, down))):
            halos.append(
                copy(
                    grown.at[pl.ds(frm, STEPS)],
                    grown.at[pl.ds(at, STEPS)],
                    halo_s.at[2 * n + side],
                    halo_r.at[2 * n + side],
                    "slab",
                    to,
                )
            )
    for item in halos:
        item.start()
    lax.fori_loop(EARLY, MIDDLE, every, 0)
    width = observed // slabs
    inverse_var = 1.0 / (os_ref[...] * os_ref[...])
    first_line = lax.broadcasted_iota(jnp.int32, (8, observed), 0) == 0
    observations = jnp.where(first_line, inverse_var, ov_ref[...])
    observations = pltpu.roll(observations, lax.rem(observed - width * slab, observed), 1)
    inside = lax.broadcasted_iota(jnp.int32, (8, LANES), 1) < width
    observations = jnp.where(inside, observations[:, 0:LANES], 0.0)

    for item in halos:
        item.wait_recv()
    head, perm, source = hx[...], cx[...], wx[...]
    open_first = jnp.where(slab == 0, 0.0, 1.0)
    open_last = jnp.where(slab == slabs - 1, 0.0, 1.0)
    for k in range(STEPS):
        head = advance(head, perm, source, open_first, open_last, k, rows)
        perm, source = perm[1:-1], source[1:-1]
    fore[...] = head
    w_ref[...] = jnp.zeros_like(w_ref)
    for i in range(rows):
        high, low = split(head[i])
        w_ref[0:local, cols * i : cols * i + cols] = high
        w_ref[16 : 16 + local, cols * i : cols * i + cols] = low

    shares = LANES // width
    each = local // shares
    line = lax.broadcasted_iota(jnp.int32, (64, 32), 0)
    col = lax.broadcasted_iota(jnp.int32, (64, 32), 1)
    wanted = lax.rem(line // 8, 4) * each + lax.rem(line, 8) + (line // 32) * 16
    valid = lax.rem(line, 8) < each
    gather = jnp.where(valid & (col == wanted), 1.0, 0.0).astype(BF16)
    wo_ref[...] = jnp.dot(gather, w_ref[...], preferred_element_type=F32).astype(BF16)
    lane = lax.broadcasted_iota(jnp.int32, (8, LANES), 1) // width
    order = [lax.rem(n + slab // (slabs // obs_blocks), obs_blocks) for n in range(obs_blocks)]

    def seen(b):
        total = jnp.dot(wo_ref[...], ohi[b], preferred_element_type=F32)
        total += jnp.dot(wo_ref[...], olo[b], preferred_element_type=F32)
        return total[0:32] + total[32:64]

    ahead = seen(order[0])
    for n, b in enumerate(order):
        total = ahead
        if n + 1 < obs_blocks:
            ahead = seen(order[n + 1])
        for half in range(BLOCK // LANES):
            block = total[:, LANES * half : LANES * half + LANES]
            for u in range(shares):
                chunk = None
                for g in range(shares):
                    piece = pltpu.roll(block[8 * g : 8 * g + 8], (width * (g - u)) % LANES, 1)
                    chunk = piece if g == 0 else jnp.where(lane == g, piece, chunk)
                po[(b * (BLOCK // LANES) + half) * shares + u] = chunk[0:4]
        count = slabs // obs_blocks

        def send(i, carry, b=b):
            to = b * count + lax.rem(i + slab, count)

            @pl.when(to != slab)
            def _():
                send_obs.one(to)

            return carry

        lax.fori_loop(0, count, send, 0)
    send_fore.start()
    ro[slab] = po[slab]

    def whole(n, carry):
        b = lax.rem(n + slab // 2, blocks)
        total = jnp.dot(w_ref[...], khi[b], preferred_element_type=F32)
        total += jnp.dot(w_ref[...], klo[b], preferred_element_type=F32)
        total = total[0:16] + total[16:32]
        for half in range(BLOCK // LANES):
            part[b * (BLOCK // LANES) + half] = total[0:local, LANES * half : LANES * half + LANES]
        return carry

    def send_parts(n, carry):
        to = lax.rem(n + (slab // 2) * (BLOCK // LANES), slabs)

        @pl.when(to != slab)
        def _():
            send_part.one(to)

        return carry

    burst = FIRST * (BLOCK // LANES)
    lax.fori_loop(0, FIRST, whole, 0)
    lax.fori_loop(0, burst, send_parts, 0)
    lax.fori_loop(MIDDLE, LATE, every, 0)
    send_obs.arrive()
    total = total_of(ro)
    mine[...] = total
    ao[member] = total
    send_mine.start()
    lax.fori_loop(LATE, blocks, every, 0)
    lax.fori_loop(FIRST, SECOND, whole, 0)
    send_obs.drain()
    send_mine.arrive()
    lane = lax.broadcasted_iota(jnp.int32, (4, LANES), 1)
    for n in range(groups):
        tile = ao[n]
        for g in range(shares):
            piece = tile if g == 0 else pltpu.roll(tile, LANES - width * g, 1)
            at = local * n + each * g
            flat[at : at + each, :] = jnp.where(lane < width, piece, 0.0)[0:each]
    predicted = flat[...]
    centre = jnp.sum(predicted, axis=0, keepdims=True) * (1.0 / members)
    anomaly = predicted - centre
    weight = observations[0:1]
    gram = mm_nt(anomaly, anomaly * weight)
    rhs = mm_nt(jnp.broadcast_to(weight * (observations[1:2] - centre), (8, LANES)), anomaly)
    size = members // 3
    top = jnp.concatenate([gram[0:size, 0:size], gram[2 * size :, 2 * size :]], axis=1)
    pieces = [top, gram[size:, 0 : 2 * size], rhs[:, 0:LANES]]
    pieces.append(jnp.concatenate([rhs[:, LANES:], jnp.zeros((8, 2 * LANES - members), F32)], axis=1))
    pieces.append(jnp.zeros((slabs * height - members - 16, LANES), F32))
    gpart[...] = jnp.concatenate(pieces, axis=0).reshape(slabs, height, LANES)
    far_first("slab", lambda to: pl.when(to < owners)(lambda: send_gram.one(to)))
    lax.fori_loop(SECOND, blocks, whole, 0)
    lax.fori_loop(burst, slabs, send_parts, 0)
    rs[slab] = part[slab]
    send_mine.drain()

    @pl.when(slab < owners)
    def _():
        gred[slab] = gpart[slab]
        send_gram.arrive()
        gall[slab] = total_of(gred)
        send_sum.start()

    def owned(wait):
        if owners == slabs:
            wait(owners - 1)
        else:
            pl.when(slab < owners)(lambda: wait(owners - 1))
            pl.when(slab >= owners)(lambda: wait(owners))

    owned(lambda n: send_gram.every(n).wait_send())
    send_fore.arrive()
    pile[member] = fore[member]
    for n in range(groups):
        flat[local * n : local * n + local, :] = pile[n]
    spread = flat[...]
    centre = jnp.sum(spread, axis=0, keepdims=True) * (1.0 / members)
    spread = spread - centre
    send_part.arrive()
    total = jnp.concatenate([total_of(rs), jnp.zeros((LANES - local, LANES), F32)], axis=0)
    turned[...] = total.T.reshape(groups, own, LANES)
    owned(lambda n: send_sum.every(n).wait_recv())
    send_own.start()
    got[member] = turned[member]
    packed = gall[...].reshape(slabs * height, LANES)
    rhs = jnp.concatenate(
        [packed[members : members + 1], packed[members + 8 : members + 9]], axis=1
    )[:, 0:members]
    mix = transform(packed[0:members], rhs, members)
    flat[...] = centre + mm(mix, spread)
    for n in range(groups):
        snd[n] = flat[local * n : local * n + local, :]
    send_back.start()
    back[member] = snd[member]
    send_own.arrive()
    total = jnp.zeros((own, 2 * LANES), F32)
    for n in range(groups):
        tile = jnp.concatenate([got[n], jnp.zeros((own, LANES), F32)], axis=1)
        total += tile if n == 0 else pltpu.roll(tile, local * n, 1)
    own_ref[...] = total[:, 0:members]
    for item in halos:
        item.wait_send()
    send_fore.drain()
    send_part.drain()
    pl.when(slab < owners)(send_sum.drain)
    send_own.drain()
    send_back.arrive()
    for i in range(rows):
        ret_ref[:, i, :] = back[i]
    send_back.drain()


def shards(
    fluid_head_start,
    conductivity_matrix,
    well_rates,
    cell_layer,
    pixel_coords,
    obs_index,
    obs_value,
    obs_sigma,
):
    local, rows, cols = fluid_head_start.shape
    groups = lax.axis_size("member")
    slabs = lax.axis_size("slab")
    members = local * groups
    pixels = pixel_coords.shape[1]
    observed = obs_index.shape[0]
    own = pixels // (groups * slabs)
    height = 256 // slabs
    place = pl.BlockSpec(memory_space=pltpu.VMEM)
    tall = rows + 2 * STEPS

    def f32(*shape):
        return pltpu.VMEM(shape, F32)

    def bf16(*shape):
        return pltpu.VMEM(shape, BF16)

    def pair(shape):
        return [pltpu.SemaphoreType.DMA(shape)] * 2

    body = lambda *refs: cycle_kernel(rows * slabs, *refs)
    arguments = (
        fluid_head_start,
        conductivity_matrix,
        well_rates,
        cell_layer,
        pixel_coords,
        obs_index[None],
        obs_value[None],
        obs_sigma[None],
    )
    returned, own_part = pl.pallas_call(
        body,
        name="cycle",
        out_shape=(
            jax.ShapeDtypeStruct((local, rows, cols), F32),
            jax.ShapeDtypeStruct((own, members), F32),
        ),
        in_specs=[pl.BlockSpec(memory_space=pltpu.HBM)] * 8,
        out_specs=(place, place),
        scratch_shapes=[
            f32(tall, local, cols),
            f32(tall, local, cols),
            f32(tall, 1, cols),
            f32(rows, local, cols),
            bf16(32, rows * cols),
            f32(rows, cols, LANES),
            f32(rows, cols, LANES),
            bf16(pixels // BLOCK, rows * cols, BLOCK),
            bf16(pixels // BLOCK, rows * cols, BLOCK),
            bf16(observed // BLOCK, rows * cols, BLOCK),
            bf16(observed // BLOCK, rows * cols, BLOCK),
            f32(2 * pixels // LANES, LANES),
            f32(8, observed),
            f32(2, pixels),
            bf16(64, rows * cols),
            f32(slabs, 4, LANES),
            f32(slabs, 4, LANES),
            f32(4, LANES),
            f32(groups, 4, LANES),
            f32(members, LANES),
            f32(slabs, local, LANES),
            f32(slabs, local, LANES),
            f32(groups, own, LANES),
            f32(groups, own, LANES),
            f32(slabs, height, LANES),
            f32(slabs, height, LANES),
            f32(slabs, height, LANES),
            f32(groups, local, cols),
            f32(groups, local, cols),
            f32(groups, local, cols),
            *pair((6,)),
            *(pair(()) * 8),
            *(pltpu.VMEM(value.shape, value.dtype) for value in arguments),
            pltpu.SemaphoreType.DMA((len(arguments),)),
        ],
        compiler_params=pltpu.CompilerParams(
            collective_id=0, has_side_effects=True, vmem_limit_bytes=52 * 1024 * 1024
        ),
    )(*(pltpu.with_memory_space_constraint(value, pltpu.HBM) for value in arguments))
    return (returned, own_part)


def solution(mesh):
    return jax.shard_map(
        shards,
        mesh=mesh,
        in_specs=(
            P("member", "slab", None),
            P("member", "slab", None),
            P("slab", None),
            P("slab", None),
            P(),
            P(),
            P(),
            P(),
        ),
        out_specs=(P("member", "slab", None), P(("member", "slab"), None)),
        check_vma=False,
    )
```
